256 devices in a mesh: seq: 32 (over z, y), head: 8 (over x, core).
Axes of the slice: x: 4, y: 4, z: 8, core: 2. Of those that a mesh axis runs over, the one named last changes fastest.
Arguments:
- queries: bfloat16 [16384, 4096], P('seq', 'head'), may hold values from -6 to 6
- keys: bfloat16 [16384, 4096], P('seq', 'head'), may hold values from -6 to 6
- values: bfloat16 [16384, 4096], P('seq', 'head'), may hold values from -6 to 6
- rates: float32 [8, 16384], P('head', 'seq'), may hold values from 0.005 to 0.05
- gain: float32 [4096], P('head'), may hold values from 0.1 to 1.9
- cotangent: bfloat16 [16384, 4096], P('seq', 'head'), may hold values from -6 to 6
- fast_init: float32 [8, 3, 512, 512], P('head'), may hold values from -60 to 60
- first_moment: float32 [8, 3, 512, 512], P('head', None, 'seq'), may hold values from -6 to 6
- second_moment: float32 [8, 3, 512, 512], P('head', None, 'seq'), may hold values from 0.5 to 4
Outputs:
- layer_out: bfloat16 [16384, 4096], P('seq', 'head')
- new_weights: float32 [8, 3, 512, 512], P('head', None, 'seq')
- new_first: float32 [8, 3, 512, 512], P('head', None, 'seq')
- new_second: float32 [8, 3, 512, 512], P('head', None, 'seq')
The draws below stay inside these ranges and needn't reach their ends.
All inputs are finite; a program needn't handle non-finite values.
Results may differ from the reference program's by a relative error of at most 0.015.
Values may be sent and summed in bfloat16 or wider, within the bound.
No kernel may reach another device: no remote copies, remote signals or barrier semaphores. Data moves between devices by JAX's collectives and lax.ppermute only.
A program may use at most 64 MiB of HBM per device.

```python
import math
import jax
import jax.numpy as jnp
from jax import lax

HEADS = 8
DH = 512
FH = 512
WIN = 256
WIDTH = 4096
TOKENS = 16384


def draw_queries(key, part):
    base = jax.random.truncated_normal(jax.random.fold_in(key, 1), -6.0, 6.0, (TOKENS, WIDTH), jnp.float32)
    return base.astype(jnp.bfloat16)


def draw_keys(key, part):
    base = jax.random.truncated_normal(jax.random.fold_in(key, 2), -6.0, 6.0, (TOKENS, WIDTH), jnp.float32)
    return base.astype(jnp.bfloat16)


def draw_fast_init(key, part):
    key_one, key_two = jax.random.split(jax.random.fold_in(key, 3))
    base = jax.random.truncated_normal(key_one, -4.0, 4.0, (HEADS, 3, DH, FH), jnp.float32)
    head_factor = 3.0 ** (jnp.arange(HEADS, dtype=jnp.float32) / max(HEADS - 1, 1) / 3.0)
    top_log = math.log(4.0)
    row_factor = jnp.exp(jax.random.uniform(key_two, (HEADS, DH), jnp.float32, 0.0, top_log))
    factor = jnp.where(jnp.arange(3)[None, :, None] == 2, row_factor[:, None, :], 1.0)
    return base * head_factor[:, None, None, None] * factor[:, :, :, None]


def block_levels(own_key, extent, shards, least, high):
    level = 1.0
    for position, parts in shards:
        steps = jax.random.uniform(jax.random.fold_in(jax.random.fold_in(own_key, 6), position), (parts,), jnp.float32, least / len(shards), high / len(shards))
        level = level * jnp.repeat(jnp.exp(steps), extent[position] // parts).reshape((-1,) + (1,) * (len(extent) - 1 - position))
    return level


def gaussian(key, extent, scale, bound, pieces=(), kind=jnp.bfloat16):
    drawn = jax.random.normal(key, extent, jnp.float32) * scale
    if len(pieces) > 0:
        drawn = block_levels(key, extent, pieces, -0.22, 0.18) * drawn
    return jnp.clip(drawn, min=-bound, max=bound).astype(kind)


def setup_inputs(seed: int = 0) -> dict:
    key_list = jax.random.split(jax.random.key(seed), 10)
    return {
        "queries": draw_queries(jax.random.fold_in(key_list[9], 71), 0),
        "keys": draw_keys(jax.random.fold_in(key_list[9], 71), 0),
        "values": gaussian(key_list[2], (TOKENS, WIDTH), 1.0, 6.0, ((0, 32), (1, 8))),
        "rates": jnp.clip(jnp.exp(math.log(0.05) - 2.3025851 * jax.random.uniform(key_list[3], (HEADS, TOKENS), jnp.float32) ** block_levels(key_list[3], (HEADS, TOKENS), ((0, 8), (1, 32)), -0.2, 0.2)), 0.005, 0.05),
        "gain": jnp.clip(1.0 + 0.18 * jax.random.normal(key_list[4], (WIDTH,), jnp.float32), 0.1, 1.9),
        "cotangent": gaussian(key_list[5], (TOKENS, WIDTH), 1.0, 6.0, ((0, 32), (1, 8))),
        "fast_init": draw_fast_init(jax.random.fold_in(key_list[9], 71), 0),
        "first_moment": gaussian(key_list[7], (HEADS, 3, DH, FH), 1.0, 6.0, ((0, 8), (2, 32)), jnp.float32),
        "second_moment": jnp.clip(jnp.exp(math.log(4.0) - 2.0794415 * jax.random.uniform(key_list[8], (HEADS, 3, DH, FH), jnp.float32) ** block_levels(key_list[8], (HEADS, 3, DH, FH), ((0, 8), (2, 32)), -0.2, 0.2)), 0.5, 4.0),
    }


highest = lax.Precision.HIGHEST
beta_one = 0.9
beta_two = 0.95
adam_rate = 0.02

def fast_apply(weights, inputs):
    scale_in = weights.shape[1] ** (-0.5)
    scale_hid = weights.shape[2] ** (-0.5)
    first_pre = jnp.dot(inputs, weights[0], precision=highest) * scale_in
    third_pre = jnp.dot(inputs, weights[1], precision=highest) * scale_in
    hidden = jax.nn.silu(first_pre) * third_pre
    return lax.dot_general(hidden, weights[2], (((1,), (1,)), ((), ())), precision=highest) * scale_hid

def inner_loss(weights, key_rows, value_rows, rate_rows):
    return -jnp.sum(rate_rows[:, None] * fast_apply(weights, key_rows) * value_rows)

def inner_grad(weights, key_rows, value_rows, rate_rows):
    return jax.grad(inner_loss)(weights, key_rows, value_rows, rate_rows)

def renorm(weights, updated):
    target = jnp.sqrt(lax.optimization_barrier(jnp.mean(weights * weights, axis=-1, keepdims=True)))
    return updated * (target / jnp.sqrt(lax.optimization_barrier(jnp.mean(updated * updated, axis=-1, keepdims=True)) + 1e-06))

def second_order(weights, key_rows, value_rows, rate_rows, direction):
    _, pull_back = jax.vjp(lambda matrix: inner_grad(matrix, key_rows, value_rows, rate_rows), weights)
    return pull_back(direction)[0]

def adam_step(weights, gradient, first_moment, second_moment):
    first_next = beta_one * first_moment + (1.0 - beta_one) * gradient
    second_next = beta_two * second_moment + (1.0 - beta_two) * gradient * gradient
    first_hat = first_next / (1.0 - beta_one ** 10)
    second_hat = second_next / (1.0 - beta_two ** 10)
    return (weights - adam_rate * first_hat / (jnp.sqrt(second_hat) + 1e-08), first_next, second_next)

def window_attention(queries, keys, values):
    block_rows = math.gcd(TOKENS, 512)
    keys_padded = jnp.concatenate([jnp.zeros((WIN, WIDTH), keys.dtype), keys], axis=0)
    values_padded = jnp.concatenate([jnp.zeros((WIN, WIDTH), values.dtype), values], axis=0)

    def one_block(block_start):
        query_block = lax.dynamic_slice_in_dim(queries, block_start, block_rows, 0).astype(jnp.float32).reshape(block_rows, HEADS, DH)
        key_block = lax.dynamic_slice_in_dim(keys_padded, block_start, block_rows + WIN, 0).astype(jnp.float32).reshape(block_rows + WIN, HEADS, DH)
        value_block = lax.dynamic_slice_in_dim(values_padded, block_start, block_rows + WIN, 0).astype(jnp.float32).reshape(block_rows + WIN, HEADS, DH)
        scores = jnp.einsum('qhd,khd->hqk', query_block, key_block) * DH ** (-0.5)
        query_pos = block_start + jnp.arange(block_rows, dtype=jnp.int32)
        key_pos = block_start - WIN + jnp.arange(block_rows + WIN, dtype=jnp.int32)
        in_window = (key_pos[None, :] <= query_pos[:, None]) & (key_pos[None, :] > query_pos[:, None] - WIN) & (key_pos[None, :] >= 0)
        scores = jnp.where(in_window[None], scores, -1e+30)
        row_max = lax.optimization_barrier(jnp.max(scores, axis=-1, keepdims=True))
        expo = jnp.exp(scores - row_max)
        probs = (expo / lax.optimization_barrier(jnp.sum(expo, axis=-1, keepdims=True))).astype(jnp.bfloat16)
        probs = lax.optimization_barrier(probs).astype(jnp.float32)
        return jnp.einsum('hqk,khd->qhd', probs, value_block).reshape(block_rows, WIDTH)
    starts = (jnp.arange(TOKENS // block_rows) * block_rows).astype(jnp.int32)
    return lax.map(one_block, starts).reshape(TOKENS, WIDTH)

def reference(queries, keys, values, rates, gain, cotangent, fast_init, first_moment, second_moment):
    attention = window_attention(queries, keys, values)

    def split_heads(array):
        return array.astype(jnp.float32).reshape(TOKENS, HEADS, DH).transpose(1, 0, 2)
    query_h = split_heads(queries)
    key_h = split_heads(keys)
    value_h = split_heads(values)
    cot_h = split_heads(cotangent)

    def forward_head(inputs):
        weights, key_rows, value_rows, rate_rows, query_rows = inputs
        updated = weights - inner_grad(weights, key_rows, value_rows, rate_rows)
        return fast_apply(renorm(weights, updated), query_rows)
    fast_out = lax.map(forward_head, (fast_init, key_h, value_h, rates, query_h))
    gain_h = gain.reshape(HEADS, 1, DH)
    sum_squares = lax.optimization_barrier(jnp.sum(fast_out * fast_out, axis=(0, 2)))
    inner_prod = lax.optimization_barrier(jnp.sum(cot_h * gain_h * fast_out, axis=(0, 2)))
    root = jnp.sqrt(sum_squares / WIDTH + 1e-06)
    normed = fast_out / root[None, :, None] * gain_h
    layer_out = (attention + normed.transpose(1, 0, 2).reshape(TOKENS, WIDTH)).astype(jnp.bfloat16)
    d_fast = gain_h * cot_h / root[None, :, None] - fast_out * (inner_prod / (WIDTH * root ** 3))[None, :, None]

    def backward_head(inputs):
        weights, key_rows, value_rows, rate_rows, query_rows, d_rows = inputs
        updated = weights - inner_grad(weights, key_rows, value_rows, rate_rows)
        renormed, pull_norm = jax.vjp(renorm, weights, updated)
        _, pull_apply = jax.vjp(lambda matrix: fast_apply(matrix, query_rows), renormed)
        d_renormed = pull_apply(d_rows)[0]
        d_weights, d_updated = pull_norm(d_renormed)
        return d_weights + d_updated - second_order(weights, key_rows, value_rows, rate_rows, d_updated)
    gradient = lax.map(backward_head, (fast_init, key_h, value_h, rates, query_h, d_fast))
    new_weights, new_first, new_second = adam_step(fast_init, gradient, first_moment, second_moment)
    return (layer_out, new_weights, new_first, new_second)
```

```python
import jax
import jax.numpy as jnp
from jax import lax
from jax.sharding import Mesh
from jax.sharding import PartitionSpec as P

WIN = 256
WIDTH = 4096
SEQ = ("z", "y")
HEAD = ("x", "c")
NY = 4
NZ = 8
beta_one = 0.9
beta_two = 0.95
adam_rate = 0.02
bf16 = jnp.bfloat16
f32 = jnp.float32


def shifted(value, axis, step):
    count = lax.axis_size(axis)
    return lax.ppermute(value, axis, [(i, (i + step) % count) for i in range(count)])


def mm(a, b, ca, cb):
    return lax.dot_general(
        a.astype(bf16), b.astype(bf16), (((ca,), (cb,)), ((), ())), preferred_element_type=f32
    )


def rolled(array, axis, start, size):
    twice = jnp.concatenate([array, array], axis=axis)
    return lax.dynamic_slice_in_dim(twice, start, size, axis)


def reduce_rows(grads, z, y):
    blocks = grads.astype(bf16).reshape(3, NZ, NY, -1, grads.shape[2])
    parts = [
        lax.dynamic_index_in_dim(blocks, (y + i) % NY, 2, keepdims=False) for i in range(NY)
    ]
    got = [shifted(parts[i], "y", i) for i in (2, 1, 3)]
    total = parts[0].astype(f32) + got[0].astype(f32) + got[1].astype(f32) + got[2].astype(f32)
    pieces = [
        lax.dynamic_index_in_dim(total, (z + j) % NZ, 1, keepdims=False) for j in range(NZ)
    ]
    got = [shifted(pieces[j].astype(bf16), "z", j) for j in (4, 3, 5, 2, 6, 1, 7)]
    out = pieces[0]
    for piece in got:
        out = out + piece.astype(f32)
    return out


def gather_rows(rows, z, y):
    pieces = [rows] + [shifted(rows, "z", -j) for j in range(1, NZ)]
    block = rolled(jnp.stack(pieces, axis=1), 1, NZ - z, NZ)
    got = {i: shifted(block, "y", -i) for i in (2, 1, 3)}
    blocks = jnp.stack([block, got[1], got[2], got[3]], axis=2)
    return rolled(blocks, 2, NY - y, NY).reshape(3, -1, rows.shape[2])


def gates(pre):
    sig = 1.0 / (1.0 + jnp.exp(-pre))
    d_sig = sig * (1.0 - sig)
    return pre * sig, sig + pre * d_sig, d_sig * (2.0 + pre * (1.0 - 2.0 * sig))


def attention_of(queries, keys, values, tail_k, tail_v, seq_index):
    tok_rows, head_dim = queries.shape
    key_all = jnp.concatenate([tail_k, keys], axis=0)
    value_all = jnp.concatenate([tail_v, values], axis=0)
    scores = lax.dot_general(
        queries, key_all, (((1,), (1,)), ((), ())), preferred_element_type=f32
    ) * head_dim ** (-0.5)
    query_pos = jnp.arange(tok_rows, dtype=jnp.int32)[:, None]
    key_pos = jnp.arange(tok_rows + WIN, dtype=jnp.int32)[None, :] - WIN
    in_window = (
        (key_pos <= query_pos)
        & (key_pos > query_pos - WIN)
        & (key_pos + seq_index * tok_rows >= 0)
    )
    scores = jnp.where(in_window, scores, -1e30)
    row_max = jnp.max(scores, axis=-1, keepdims=True)
    expo = jnp.exp(scores - row_max)
    probs = (expo / jnp.sum(expo, axis=-1, keepdims=True)).astype(bf16)
    return jnp.dot(probs, value_all, preferred_element_type=f32)


def row_scale(weights, updated):
    target = jnp.sqrt(jnp.mean(weights * weights, axis=-1, keepdims=True))
    return target / jnp.sqrt(jnp.mean(updated * updated, axis=-1, keepdims=True) + 1e-06)


def renorm(weights, updated):
    return updated * row_scale(weights, updated)


def adam_step(weights, gradient, first_moment, second_moment):
    first_next = beta_one * first_moment + (1.0 - beta_one) * gradient
    second_next = beta_two * second_moment + (1.0 - beta_two) * gradient * gradient
    first_hat = first_next / (1.0 - beta_one**10)
    second_hat = second_next / (1.0 - beta_two**10)
    return (
        weights - adam_rate * first_hat / (jnp.sqrt(second_hat) + 1e-08),
        first_next,
        second_next,
    )


def local(queries, keys, values, rates, gain, cotangent, fast_init, first_moment, second_moment):
    tok_rows, dim = queries.shape
    z = lax.axis_index("z")
    y = lax.axis_index("y")
    seq_index = z * NY + y
    scale = dim ** (-0.5)
    weights = fast_init[0]

    last = NY * NZ - 1
    pairs = [(i, i + 1) for i in range(last)]
    tails = [lax.ppermute(a[tok_rows - WIN :], SEQ, pairs) for a in (keys, values)]

    first_pre = scale * mm(keys, weights[0], 1, 0)
    third_pre = scale * mm(keys, weights[1], 1, 0)
    gate, gate1, gate2 = gates(first_pre)
    factor = (-scale) * rates[0][:, None]
    err = factor * values.astype(f32)
    back = factor * mm(values, weights[2], 1, 0)
    grads = jnp.stack(
        [
        scale * mm(keys, back * third_pre * gate1, 0, 0),
        scale * mm(keys, back * gate, 0, 0),
        mm(err, gate * third_pre, 0, 0),
        ]
    )
    update_rows = reduce_rows(grads, z, y)
    rows = dim // (NY * NZ)
    init_rows = lax.dynamic_slice_in_dim(weights, seq_index * rows, rows, 1)
    moved_rows = init_rows - update_rows
    renormed = gather_rows(renorm(init_rows, moved_rows).astype(bf16), z, y)

    first_q = scale * mm(queries, renormed[0], 1, 0)
    third_q = scale * mm(queries, renormed[1], 1, 0)
    gate_q, gate1_q, _ = gates(first_q)
    hidden_q = gate_q * third_q
    fast_out = scale * mm(hidden_q, renormed[2], 1, 1)
    weighted = cotangent.astype(f32) * gain[None, :]
    sums = jnp.stack([jnp.sum(fast_out * fast_out, axis=1), jnp.sum(weighted * fast_out, axis=1)])
    sums = sums + shifted(sums, "c", 1)
    sums = sums + shifted(sums, "x", 1) + shifted(sums, "x", 2) + shifted(sums, "x", 3)
    root = jnp.sqrt(sums[0] / WIDTH + 1e-06)[:, None]
    coef = sums[1][:, None] / (WIDTH * root**3)
    d_fast = weighted / root - fast_out * coef
    err_q = scale * d_fast
    back_q = mm(err_q, renormed[2], 1, 0)
    grads = jnp.stack(
        [
        scale * mm(queries, back_q * third_q * gate1_q, 0, 0),
        scale * mm(queries, back_q * gate_q, 0, 0),
        mm(err_q, hidden_q, 0, 0),
        ]
    )
    cot_rows = reduce_rows(grads, z, y)
    _, pull_norm = jax.vjp(renorm, init_rows, moved_rows)
    d_init_rows, d_moved_rows = pull_norm(cot_rows)
    local_part = d_init_rows + d_moved_rows
    direction = gather_rows(d_moved_rows.astype(bf16), z, y)

    first_dot = scale * mm(keys, direction[0], 1, 0)
    third_dot = scale * mm(keys, direction[1], 1, 0)
    back_dot = factor * mm(values, direction[2], 1, 0)
    bent = gate1 * first_dot
    grads = jnp.stack(
        [
        scale
        * mm(
            keys,
            back_dot * third_pre * gate1
            + back * third_dot * gate1
            + back * third_pre * gate2 * first_dot,
            0,
            0,
        ),
        scale * mm(keys, back_dot * gate + back * bent, 0, 0),
        mm(err, bent * third_pre + gate * third_dot, 0, 0),
        ]
    )
    grad_rows = local_part - reduce_rows(grads, z, y)

    attention = attention_of(queries, keys, values, tails[0], tails[1], seq_index)
    normed = fast_out / root * gain[None, :]
    layer_out = (attention + normed).astype(bf16)
    new = adam_step(init_rows, grad_rows, first_moment[0], second_moment[0])
    return (layer_out, new[0][None], new[1][None], new[2][None])


def solution(mesh):
    split = Mesh(mesh.devices.reshape(NZ, NY, 4, 2), ("z", "y", "x", "c"))
    placed = (
        P(SEQ, HEAD),
        P(SEQ, HEAD),
        P(SEQ, HEAD),
        P(HEAD, SEQ),
        P(HEAD),
        P(SEQ, HEAD),
        P(HEAD, None, None, None),
        P(HEAD, None, SEQ, None),
        P(HEAD, None, SEQ, None),
    )
    return jax.shard_map(
        local,
        mesh=split,
        in_specs=placed,
        out_specs=(
            P(SEQ, HEAD),
            P(HEAD, None, SEQ, None),
            P(HEAD, None, SEQ, None),
            P(HEAD, None, SEQ, None),
        ),
        check_vma=False,
    )
```

```python
import jax
import jax.numpy as jnp
from jax import lax
from jax.sharding import Mesh
from jax.sharding import PartitionSpec as P

WIN = 256
WIDTH = 4096
Z = ("zh", "zl")
SEQ = ("zh", "zl", "y")
HEAD = ("x", "c")
NY = 4
NZ = 8
beta_one = 0.9
beta_two = 0.95
adam_rate = 0.02
bf16 = jnp.bfloat16
f32 = jnp.float32


def mm(a, b, ca, cb):
    return lax.dot_general(
        a.astype(bf16), b.astype(bf16), (((ca,), (cb,)), ((), ())), preferred_element_type=f32
    )


def swapped(parts, axes):
    return lax.all_to_all(parts, axes, split_axis=0, concat_axis=0, tiled=True)


def reduce_rows(grads):
    count, _, width = grads.shape
    blocks = grads.astype(bf16).reshape(count, NZ, NY, -1, width)
    got = swapped(jnp.transpose(blocks, (2, 0, 1, 3, 4)), "y")
    total = jnp.sum(got.astype(f32), axis=0)
    got = swapped(jnp.transpose(total.astype(bf16), (1, 0, 2, 3)), Z)
    return jnp.sum(got.astype(f32), axis=0)


def gather_rows(rows):
    count, _, width = rows.shape
    block = swapped(jnp.broadcast_to(rows, (4, *rows.shape)), "zh")
    got = swapped(jnp.broadcast_to(block, (8, *block.shape)), ("zl", "y"))
    got = got.reshape(2, NY, 4, *rows.shape)
    return jnp.transpose(got, (3, 2, 0, 1, 4, 5)).reshape(count, -1, width)


def gates(pre):
    sig = 1.0 / (1.0 + jnp.exp(-pre))
    d_sig = sig * (1.0 - sig)
    return pre * sig, sig + pre * d_sig, d_sig * (2.0 + pre * (1.0 - 2.0 * sig))


def attention_of(queries, keys, values, tail_k, tail_v, seq_index):
    tok_rows, head_dim = queries.shape
    key_all = jnp.concatenate([tail_k, keys], axis=0)
    value_all = jnp.concatenate([tail_v, values], axis=0)
    scores = lax.dot_general(
        queries, key_all, (((1,), (1,)), ((), ())), preferred_element_type=f32
    ) * head_dim ** (-0.5)
    query_pos = jnp.arange(tok_rows, dtype=jnp.int32)[:, None]
    key_pos = jnp.arange(tok_rows + WIN, dtype=jnp.int32)[None, :] - WIN
    in_window = (
        (key_pos <= query_pos)
        & (key_pos > query_pos - WIN)
        & (key_pos + seq_index * tok_rows >= 0)
    )
    scores = jnp.where(in_window, scores, -1e30)
    row_max = jnp.max(scores, axis=-1, keepdims=True)
    expo = jnp.exp(scores - row_max)
    probs = (expo / jnp.sum(expo, axis=-1, keepdims=True)).astype(bf16)
    return jnp.dot(probs, value_all, preferred_element_type=f32)


def row_scale(weights, updated):
    target = jnp.sqrt(jnp.mean(weights * weights, axis=-1, keepdims=True))
    return target / jnp.sqrt(jnp.mean(updated * updated, axis=-1, keepdims=True) + 1e-06)


def renorm(weights, updated):
    return updated * row_scale(weights, updated)


def adam_step(weights, gradient, first_moment, second_moment):
    first_next = beta_one * first_moment + (1.0 - beta_one) * gradient
    second_next = beta_two * second_moment + (1.0 - beta_two) * gradient * gradient
    first_hat = first_next / (1.0 - beta_one**10)
    second_hat = second_next / (1.0 - beta_two**10)
    return (
        weights - adam_rate * first_hat / (jnp.sqrt(second_hat) + 1e-08),
        first_next,
        second_next,
    )


def local(queries, keys, values, rates, gain, cotangent, fast_init, first_moment, second_moment):
    tok_rows, dim = queries.shape
    z = lax.axis_index(Z)
    y = lax.axis_index("y")
    seq_index = z * NY + y
    scale = dim ** (-0.5)
    weights = fast_init[0]

    last = NY * NZ - 1
    pairs = [(i, i + 1) for i in range(last)]
    tails = [lax.ppermute(a[tok_rows - WIN :], SEQ, pairs) for a in (keys, values)]

    first_pre = scale * mm(keys, weights[0], 1, 0)
    third_pre = scale * mm(keys, weights[1], 1, 0)
    gate, gate1, gate2 = gates(first_pre)
    factor = (-scale) * rates[0][:, None]
    err = factor * values.astype(f32)
    back = factor * mm(values, weights[2], 1, 0)
    grads = jnp.stack(
        [
        scale * mm(keys, back * third_pre * gate1, 0, 0),
        scale * mm(keys, back * gate, 0, 0),
        mm(err, gate * third_pre, 0, 0),
        ]
    )
    update_rows = reduce_rows(grads)
    rows = dim // (NY * NZ)
    init_rows = lax.dynamic_slice_in_dim(weights, seq_index * rows, rows, 1)
    moved_rows = init_rows - update_rows
    renormed = gather_rows(renorm(init_rows, moved_rows).astype(bf16))

    first_q = scale * mm(queries, renormed[0], 1, 0)
    third_q = scale * mm(queries, renormed[1], 1, 0)
    gate_q, gate1_q, _ = gates(first_q)
    hidden_q = gate_q * third_q
    fast_out = scale * mm(hidden_q, renormed[2], 1, 1)
    weighted = cotangent.astype(f32) * gain[None, :]
    sums = jnp.stack([jnp.sum(fast_out * fast_out, axis=1), jnp.sum(weighted * fast_out, axis=1)])
    sums = jnp.sum(swapped(jnp.broadcast_to(sums, (8, *sums.shape)), HEAD), axis=0)
    root = jnp.sqrt(sums[0] / WIDTH + 1e-06)[:, None]
    coef = sums[1][:, None] / (WIDTH * root**3)
    d_fast = weighted / root - fast_out * coef
    err_q = scale * d_fast
    back_q = mm(err_q, renormed[2], 1, 0)
    grads = jnp.stack(
        [
        scale * mm(queries, back_q * third_q * gate1_q, 0, 0),
        scale * mm(queries, back_q * gate_q, 0, 0),
        mm(err_q, hidden_q, 0, 0),
        ]
    )
    cot_rows = reduce_rows(grads)
    _, pull_norm = jax.vjp(renorm, init_rows, moved_rows)
    d_init_rows, d_moved_rows = pull_norm(cot_rows)
    local_part = d_init_rows + d_moved_rows
    direction = gather_rows(d_moved_rows.astype(bf16))

    first_dot = scale * mm(keys, direction[0], 1, 0)
    third_dot = scale * mm(keys, direction[1], 1, 0)
    back_dot = factor * mm(values, direction[2], 1, 0)
    bent = gate1 * first_dot
    grads = jnp.stack(
        [
        scale
        * mm(
            keys,
            back_dot * third_pre * gate1
            + back * third_dot * gate1
            + back * third_pre * gate2 * first_dot,
            0,
            0,
        ),
        scale * mm(keys, back_dot * gate + back * bent, 0, 0),
        mm(err, bent * third_pre + gate * third_dot, 0, 0),
        ]
    )
    grad_rows = local_part - reduce_rows(grads)

    attention = attention_of(queries, keys, values, tails[0], tails[1], seq_index)
    normed = fast_out / root * gain[None, :]
    layer_out = (attention + normed).astype(bf16)
    new = adam_step(init_rows, grad_rows, first_moment[0], second_moment[0])
    return (layer_out, new[0][None], new[1][None], new[2][None])


def solution(mesh):
    split = Mesh(mesh.devices.reshape(4, 2, NY, 4, 2), ("zh", "zl", "y", "x", "c"))
    placed = (
        P(SEQ, HEAD),
        P(SEQ, HEAD),
        P(SEQ, HEAD),
        P(HEAD, SEQ),
        P(HEAD),
        P(SEQ, HEAD),
        P(HEAD, None, None, None),
        P(HEAD, None, SEQ, None),
        P(HEAD, None, SEQ, None),
    )
    return jax.shard_map(
        local,
        mesh=split,
        in_specs=placed,
        out_specs=(
            P(SEQ, HEAD),
            P(HEAD, None, SEQ, None),
            P(HEAD, None, SEQ, None),
            P(HEAD, None, SEQ, None),
        ),
        check_vma=False,
    )
```

```python
import jax
import jax.numpy as jnp
from jax import lax
from jax.experimental import pallas as pl
from jax.experimental.pallas import tpu as pltpu
from jax.sharding import Mesh
from jax.sharding import PartitionSpec as P

WIN = 256
WIDTH = 4096
SEQ = ("zh", "zl", "y")
PLANE = ("zl", "y")
HEAD = ("x", "c")
NY = 4
NH = 4
NP = 8
ROWS = 16
BLOCK = 128
beta_one = 0.9
beta_two = 0.95
adam_rate = 0.02
bf16 = jnp.bfloat16
f32 = jnp.float32


def mm(a, b, ca, cb):
    return lax.dot_general(
        a.astype(bf16), b.astype(bf16), (((ca,), (cb,)), ((), ())), preferred_element_type=f32
    )


def swapped(parts, axes):
    return lax.all_to_all(parts, axes, split_axis=0, concat_axis=0, tiled=True)


def copies(array, count):
    return jnp.broadcast_to(array, (count, *array.shape))


def totals(parts):
    return jnp.sum(parts.astype(f32), axis=0)


def gates(pre):
    sig = 1.0 / (1.0 + jnp.exp(-pre))
    d_sig = sig * (1.0 - sig)
    return pre * sig, sig + pre * d_sig, d_sig * (2.0 + pre * (1.0 - 2.0 * sig))


def columns(row):
    return jnp.broadcast_to(row, (128, row.shape[1])).T


def line(col):
    return jnp.broadcast_to(col, (col.shape[0], 128)).T[:1, :]


def blocks_of(count, body):
    def step(j, carry):
        body(pl.ds(pl.multiple_of(j * BLOCK, BLOCK), BLOCK))
        return carry

    lax.fori_loop(0, count // BLOCK, step, 0)


def put_grad(parts_ref, number, left, right):
    grad = mm(left[...], right[...], 0, 0).astype(bf16)
    for m in range(grad.shape[0] // ROWS):
        parts_ref[m % NP, number, m // NP] = grad[m * ROWS : (m + 1) * ROWS]


def take_matrices(parts_ref, out_ref):
    for number in range(out_ref.shape[0]):
        for m in range(out_ref.shape[1] // ROWS):
            out_ref[number, m * ROWS : (m + 1) * ROWS, :] = parts_ref[m % NP, number, m // NP]


def inner_kernel(k_ref, v_ref, r_ref, w_ref, parts_ref, p1_ref, p3_ref, b_ref, w_s, f_s, d1, d3, d2):
    tokens, dim = k_ref.shape
    scale = dim ** (-0.5)
    for m in range(3):
        w_s[m] = w_ref[m].astype(bf16)
    f_s[...] = columns(r_ref[...] * (-scale))

    def body(at):
        factor = f_s[at, :][:, :1]
        p1 = scale * mm(k_ref[at, :], w_s[0], 1, 0)
        p3 = scale * mm(k_ref[at, :], w_s[1], 1, 0)
        back = factor * mm(v_ref[at, :], w_s[2], 1, 0)
        gate, gate1, _ = gates(p1)
        p1_ref[at, :] = p1
        p3_ref[at, :] = p3
        b_ref[at, :] = back
        d1[at, :] = (scale * back * p3 * gate1).astype(bf16)
        d3[at, :] = (scale * back * gate).astype(bf16)
        d2[at, :] = (factor * gate * p3).astype(bf16)

    blocks_of(tokens, body)
    put_grad(parts_ref, 0, k_ref, d1)
    put_grad(parts_ref, 1, k_ref, d3)
    put_grad(parts_ref, 2, v_ref, d2)


def forward_kernel(got_ref, q_ref, cot_ref, gain_ref, o_ref, p1_ref, p3_ref, sums_ref, w2_ref, w_s, s_s):
    tokens, dim = q_ref.shape
    scale = dim ** (-0.5)
    take_matrices(got_ref, w_s)
    w2_ref[...] = w_s[2]

    def body(at):
        p1 = scale * mm(q_ref[at, :], w_s[0], 1, 0)
        p3 = scale * mm(q_ref[at, :], w_s[1], 1, 0)
        gate, _, _ = gates(p1)
        out = scale * mm(gate * p3, w_s[2], 1, 1)
        p1_ref[at, :] = p1
        p3_ref[at, :] = p3
        o_ref[at, :] = out
        weighted = cot_ref[at, :].astype(f32) * gain_ref[...]
        squares = jnp.sum(out * out, axis=1, keepdims=True)
        inner = jnp.sum(weighted * out, axis=1, keepdims=True)
        lane = lax.broadcasted_iota(jnp.int32, (BLOCK, 128), 1)
        s_s[at, :] = jnp.where(lane == 0, squares, inner)

    blocks_of(tokens, body)
    sums_ref[...] = jnp.broadcast_to(s_s[...].T[:2, :], sums_ref.shape)


def backward_kernel(
    sums_ref, o_ref, p1_ref, p3_ref, q_ref, cot_ref, gain_ref, w2_ref,
    parts_ref, normed_ref, s_s, d1, d3, a_s, e_s,
):
    tokens, dim = q_ref.shape
    scale = dim ** (-0.5)
    sums = jnp.sum(sums_ref[...], axis=0)
    inverse = 1.0 / jnp.sqrt(sums[:1] / WIDTH + 1e-06)
    coef = sums[1:] * inverse * inverse * inverse / WIDTH
    s_s[0] = columns(inverse)
    s_s[1] = columns(coef)

    def body(at):
        inv = s_s[0, at, :][:, :1]
        out = o_ref[at, :]
        weighted = cot_ref[at, :].astype(f32) * gain_ref[...]
        err = (scale * (weighted * inv - out * s_s[1, at, :][:, :1])).astype(bf16)
        e_s[at, :] = err
        normed_ref[at, :] = out * inv * gain_ref[...]
        back = mm(err, w2_ref[...], 1, 0)
        p3 = p3_ref[at, :]
        gate, gate1, _ = gates(p1_ref[at, :])
        d1[at, :] = (scale * back * p3 * gate1).astype(bf16)
        d3[at, :] = (scale * back * gate).astype(bf16)
        a_s[at, :] = (gate * p3).astype(bf16)

    blocks_of(tokens, body)
    put_grad(parts_ref, 0, q_ref, d1)
    put_grad(parts_ref, 1, q_ref, d3)
    put_grad(parts_ref, 2, e_s, a_s)


def second_kernel(got_ref, k_ref, v_ref, r_ref, p1_ref, p3_ref, b_ref, parts_ref, w_s, f_s, d1, d3, d2):
    tokens, dim = k_ref.shape
    scale = dim ** (-0.5)
    take_matrices(got_ref, w_s)
    f_s[...] = columns(r_ref[...] * (-scale))

    def body(at):
        factor = f_s[at, :][:, :1]
        first_dot = scale * mm(k_ref[at, :], w_s[0], 1, 0)
        third_dot = scale * mm(k_ref[at, :], w_s[1], 1, 0)
        back_dot = factor * mm(v_ref[at, :], w_s[2], 1, 0)
        p3 = p3_ref[at, :]
        back = b_ref[at, :]
        gate, gate1, gate2 = gates(p1_ref[at, :])
        bent = gate1 * first_dot
        d1[at, :] = (
            scale
            * (gate1 * (back_dot * p3 + back * third_dot) + back * p3 * gate2 * first_dot)
        ).astype(bf16)
        d3[at, :] = (scale * (back_dot * gate + back * bent)).astype(bf16)
        d2[at, :] = (factor * (bent * p3 + gate * third_dot)).astype(bf16)

    blocks_of(tokens, body)
    put_grad(parts_ref, 0, k_ref, d1)
    put_grad(parts_ref, 1, k_ref, d3)
    put_grad(parts_ref, 2, v_ref, d2)


def called(kernel, outs, scratch, *args):
    return pl.pallas_call(
        kernel,
        out_shape=[jax.ShapeDtypeStruct(*out) for out in outs],
        in_specs=[pl.BlockSpec(memory_space=pltpu.VMEM)] * len(args),
        out_specs=[pl.BlockSpec(memory_space=pltpu.VMEM)] * len(outs),
        scratch_shapes=[pltpu.VMEM(*item) for item in scratch],
    )(*args)


def to_owners(parts):
    return totals(swapped(parts, PLANE)).astype(bf16)


def attention_of(queries, keys, values, tail_k, tail_v, seq_index):
    tok_rows, head_dim = queries.shape
    key_all = jnp.concatenate([tail_k, keys], axis=0)
    value_all = jnp.concatenate([tail_v, values], axis=0)
    scores = lax.dot_general(
        queries, key_all, (((1,), (1,)), ((), ())), preferred_element_type=f32
    ) * head_dim ** (-0.5)
    query_pos = jnp.arange(tok_rows, dtype=jnp.int32)[:, None]
    key_pos = jnp.arange(tok_rows + WIN, dtype=jnp.int32)[None, :] - WIN
    in_window = (
        (key_pos <= query_pos)
        & (key_pos > query_pos - WIN)
        & (key_pos + seq_index * tok_rows >= 0)
    )
    scores = jnp.where(in_window, scores, -1e30)
    row_max = jnp.max(scores, axis=-1, keepdims=True)
    expo = jnp.exp(scores - row_max)
    probs = (expo / jnp.sum(expo, axis=-1, keepdims=True)).astype(bf16)
    return jnp.dot(probs, value_all, preferred_element_type=f32)


def renorm(weights, updated):
    target = jnp.sqrt(jnp.mean(weights * weights, axis=-1, keepdims=True))
    return updated * (
        target / jnp.sqrt(jnp.mean(updated * updated, axis=-1, keepdims=True) + 1e-06)
    )


def adam_step(weights, gradient, first_moment, second_moment):
    first_next = beta_one * first_moment + (1.0 - beta_one) * gradient
    second_next = beta_two * second_moment + (1.0 - beta_two) * gradient * gradient
    first_hat = first_next / (1.0 - beta_one**10)
    second_hat = second_next / (1.0 - beta_two**10)
    return (
        weights - adam_rate * first_hat / (jnp.sqrt(second_hat) + 1e-08),
        first_next,
        second_next,
    )


def local(queries, keys, values, rates, gain, cotangent, fast_init, first_moment, second_moment):
    tokens, dim = queries.shape
    zh = lax.axis_index("zh")
    plane = lax.axis_index(PLANE)
    weights = fast_init[0]
    full, half = ((tokens, dim), f32), ((tokens, dim), bf16)
    side = ((tokens, 128), f32)
    mats = ((3, dim, dim), bf16)
    owned = ((NP, 3, NH, ROWS, dim), bf16)
    gain_row = gain[None, :]

    last = NY * NP - 1
    pairs = [(i, i + 1) for i in range(last)]
    tails = [lax.ppermute(a[tokens - WIN :], SEQ, pairs) for a in (keys, values)]

    parts, first_pre, third_pre, back = called(
        inner_kernel, [owned, full, full, full], [mats, side, half, half, half],
        keys, values, rates, weights,
    )
    init_rows = lax.dynamic_index_in_dim(
        weights.reshape(3, NH, NP, ROWS, dim), plane, 2, keepdims=False
    )
    moved_rows = init_rows - totals(swapped(copies(to_owners(parts), NH), "zh"))
    rows = renorm(init_rows, moved_rows).astype(bf16)
    renormed = swapped(copies(rows, NP), PLANE)

    fast_out, first_q, third_q, sums, second_w = called(
        forward_kernel, [full, full, full, ((NP, 2, tokens), f32), half], [mats, side],
        renormed, queries, cotangent, gain_row,
    )
    sums = swapped(sums, HEAD)
    parts, normed = called(
        backward_kernel, [owned, full], [((2, tokens, 128), f32), half, half, half, half],
        sums, fast_out, first_q, third_q, queries, cotangent, gain_row, second_w,
    )
    cot_rows = totals(swapped(copies(to_owners(parts), NH), "zh"))
    _, pull_norm = jax.vjp(renorm, init_rows, moved_rows)
    d_init_rows, d_moved_rows = pull_norm(cot_rows)
    direction = swapped(copies(d_moved_rows.astype(bf16), NP), PLANE)

    (parts,) = called(
        second_kernel, [owned], [mats, side, half, half, half],
        direction, keys, values, rates, first_pre, third_pre, back,
    )
    second_terms = totals(swapped(jnp.moveaxis(to_owners(parts), 1, 0), "zh"))

    def own(array):
        return lax.dynamic_index_in_dim(array, zh, 1, keepdims=False)

    grad_rows = own(d_init_rows + d_moved_rows) - second_terms
    attention = attention_of(
        queries, keys, values, tails[0], tails[1], zh * NP + plane
    )
    layer_out = (attention + normed).astype(bf16)
    new = adam_step(own(init_rows), grad_rows, first_moment[0], second_moment[0])
    return (layer_out, new[0][None], new[1][None], new[2][None])


def solution(mesh):
    split = Mesh(mesh.devices.reshape(NH, 2, NY, 4, 2), ("zh", "zl", "y", "x", "c"))
    placed = (
        P(SEQ, HEAD),
        P(SEQ, HEAD),
        P(SEQ, HEAD),
        P(HEAD, SEQ),
        P(HEAD),
        P(SEQ, HEAD),
        P(HEAD, None, None, None),
        P(HEAD, None, SEQ, None),
        P(HEAD, None, SEQ, None),
    )
    return jax.shard_map(
        local,
        mesh=split,
        in_specs=placed,
        out_specs=(
            P(SEQ, HEAD),
            P(HEAD, None, SEQ, None),
            P(HEAD, None, SEQ, None),
            P(HEAD, None, SEQ, None),
        ),
        check_vma=False,
    )
```

```python
import jax
import jax.numpy as jnp
from jax import lax
from jax.experimental import pallas as pl
from jax.experimental.pallas import tpu as pltpu
from jax.sharding import Mesh
from jax.sharding import PartitionSpec as P


WIN = 256
WIDTH = 4096
SEQ = ("zh", "zl", "y")
PLANE = ("zl", "y")
HEAD = ("x", "c")
NY = 4
NH = 4
NP = 8
ROWS = 16
BLOCK = 128
VMEM_BYTES = 24 * 1024 * 1024
beta_one = 0.9
beta_two = 0.95
adam_rate = 0.02
bf16 = jnp.bfloat16
f32 = jnp.float32


def mm(a, b, ca, cb):
    return lax.dot_general(
        a.astype(bf16), b.astype(bf16), (((ca,), (cb,)), ((), ())), preferred_element_type=f32
    )


def swapped(parts, axes):
    return lax.all_to_all(parts, axes, split_axis=0, concat_axis=0, tiled=True)


def copies(array, count):
    return jnp.broadcast_to(array, (count, *array.shape))


def totals(parts):
    return jnp.sum(parts.astype(f32), axis=0)


def gates(pre):
    sig = 1.0 / (1.0 + jnp.exp(-pre))
    d_sig = sig * (1.0 - sig)
    return pre * sig, sig + pre * d_sig, d_sig * (2.0 + pre * (1.0 - 2.0 * sig))


def columns(row):
    return jnp.broadcast_to(row, (128, row.shape[1])).T


def blocks_of(count, body):
    def step(j, carry):
        body(pl.ds(pl.multiple_of(j * BLOCK, BLOCK), BLOCK))
        return carry

    lax.fori_loop(0, count // BLOCK, step, 0)


def put_grad(parts_ref, number, left, right):
    grad = mm(left[...], right[...], 0, 0).astype(bf16)
    for m in range(grad.shape[0] // ROWS):
        at = (m // NP * 3 + number) * ROWS
        parts_ref[m % NP, at : at + ROWS, :] = grad[m * ROWS : (m + 1) * ROWS]


def take_matrices(parts_ref, out_ref):
    for number in range(out_ref.shape[0]):
        for m in range(out_ref.shape[1] // ROWS):
            at = (m // NP * 3 + number) * ROWS
            out_ref[number, m * ROWS : (m + 1) * ROWS, :] = parts_ref[m % NP, at : at + ROWS, :]


def inner_kernel(k_ref, v_ref, r_ref, w_ref, parts_ref, p1_ref, p3_ref, b_ref, w_s, f_s, d1, d3, d2):
    tokens, dim = k_ref.shape
    scale = dim ** (-0.5)
    for m in range(3):
        w_s[m] = w_ref[m].astype(bf16)
    f_s[...] = columns(r_ref[...] * (-scale))

    def body(at):
        factor = f_s[at, :][:, :1]
        p1 = scale * mm(k_ref[at, :], w_s[0], 1, 0)
        p3 = scale * mm(k_ref[at, :], w_s[1], 1, 0)
        back = factor * mm(v_ref[at, :], w_s[2], 1, 0)
        gate, gate1, _ = gates(p1)
        p1_ref[at, :] = p1
        p3_ref[at, :] = p3
        b_ref[at, :] = back
        d1[at, :] = (scale * back * p3 * gate1).astype(bf16)
        d3[at, :] = (scale * back * gate).astype(bf16)
        d2[at, :] = (factor * gate * p3).astype(bf16)

    blocks_of(tokens, body)
    put_grad(parts_ref, 0, k_ref, d1)
    put_grad(parts_ref, 1, k_ref, d3)
    put_grad(parts_ref, 2, v_ref, d2)


def forward_kernel(got_ref, q_ref, cot_ref, gain_ref, o_ref, p1_ref, p3_ref, sums_ref, w2_ref, w_s, s_s):
    tokens, dim = q_ref.shape
    scale = dim ** (-0.5)
    take_matrices(got_ref, w_s)
    w2_ref[...] = w_s[2]

    def body(at):
        p1 = scale * mm(q_ref[at, :], w_s[0], 1, 0)
        p3 = scale * mm(q_ref[at, :], w_s[1], 1, 0)
        gate, _, _ = gates(p1)
        out = scale * mm(gate * p3, w_s[2], 1, 1)
        p1_ref[at, :] = p1
        p3_ref[at, :] = p3
        o_ref[at, :] = out
        weighted = cot_ref[at, :].astype(f32) * gain_ref[...]
        squares = jnp.sum(out * out, axis=1, keepdims=True)
        inner = jnp.sum(weighted * out, axis=1, keepdims=True)
        lane = lax.broadcasted_iota(jnp.int32, (BLOCK, 128), 1)
        s_s[at, :] = jnp.where(lane == 0, squares, inner)

    blocks_of(tokens, body)
    sums_ref[...] = jnp.broadcast_to(s_s[...].T[:2, :], sums_ref.shape)


def backward_kernel(
    sums_ref, o_ref, p1_ref, p3_ref, q_ref, cot_ref, gain_ref, w2_ref,
    parts_ref, normed_ref, s_s, d1, d3, a_s, e_s,
):
    tokens, dim = q_ref.shape
    scale = dim ** (-0.5)
    sums = jnp.sum(sums_ref[...], axis=0)
    inverse = 1.0 / jnp.sqrt(sums[:1] / WIDTH + 1e-06)
    coef = sums[1:] * inverse * inverse * inverse / WIDTH
    s_s[0] = columns(inverse)
    s_s[1] = columns(coef)

    def body(at):
        inv = s_s[0, at, :][:, :1]
        out = o_ref[at, :]
        weighted = cot_ref[at, :].astype(f32) * gain_ref[...]
        err = (scale * (weighted * inv - out * s_s[1, at, :][:, :1])).astype(bf16)
        e_s[at, :] = err
        normed_ref[at, :] = out * inv * gain_ref[...]
        back = mm(err, w2_ref[...], 1, 0)
        p3 = p3_ref[at, :]
        gate, gate1, _ = gates(p1_ref[at, :])
        d1[at, :] = (scale * back * p3 * gate1).astype(bf16)
        d3[at, :] = (scale * back * gate).astype(bf16)
        a_s[at, :] = (gate * p3).astype(bf16)

    blocks_of(tokens, body)
    put_grad(parts_ref, 0, q_ref, d1)
    put_grad(parts_ref, 1, q_ref, d3)
    put_grad(parts_ref, 2, e_s, a_s)


def second_kernel(got_ref, k_ref, v_ref, r_ref, p1_ref, p3_ref, b_ref, parts_ref, w_s, f_s, d1, d3, d2):
    tokens, dim = k_ref.shape
    scale = dim ** (-0.5)
    take_matrices(got_ref, w_s)
    f_s[...] = columns(r_ref[...] * (-scale))

    def body(at):
        factor = f_s[at, :][:, :1]
        first_dot = scale * mm(k_ref[at, :], w_s[0], 1, 0)
        third_dot = scale * mm(k_ref[at, :], w_s[1], 1, 0)
        back_dot = factor * mm(v_ref[at, :], w_s[2], 1, 0)
        p3 = p3_ref[at, :]
        back = b_ref[at, :]
        gate, gate1, gate2 = gates(p1_ref[at, :])
        bent = gate1 * first_dot
        d1[at, :] = (
            scale
            * (gate1 * (back_dot * p3 + back * third_dot) + back * p3 * gate2 * first_dot)
        ).astype(bf16)
        d3[at, :] = (scale * (back_dot * gate + back * bent)).astype(bf16)
        d2[at, :] = (factor * (bent * p3 + gate * third_dot)).astype(bf16)

    blocks_of(tokens, body)
    put_grad(parts_ref, 0, k_ref, d1)
    put_grad(parts_ref, 1, k_ref, d3)
    put_grad(parts_ref, 2, v_ref, d2)


def near(array):
    return pltpu.with_memory_space_constraint(array, pltpu.VMEM)


def called(kernel, outs, scratch, *args):
    return pl.pallas_call(
        kernel,
        out_shape=outs,
        in_specs=[pl.BlockSpec(memory_space=pltpu.VMEM)] * len(args),
        out_specs=[pl.BlockSpec(memory_space=pltpu.VMEM)] * len(outs),
        scratch_shapes=[pltpu.VMEM(*item) for item in scratch],
        compiler_params=pltpu.CompilerParams(vmem_limit_bytes=VMEM_BYTES),
    )(*args)


def reduce_rows(parts):
    width = parts.shape[2]
    some = swapped(parts, PLANE)
    some = totals(some).astype(bf16)
    got = swapped(some.reshape(NH, 3 * ROWS, width), "zh")
    return totals(got).reshape(3, ROWS, width)


def gather_rows(rows):
    width = rows.shape[2]
    some = swapped(copies(rows.reshape(3 * ROWS, width), NH), "zh")
    return swapped(copies(some.reshape(-1, width), NP), PLANE)


def attention_of(queries, keys, values, tail_k, tail_v, seq_index):
    tok_rows, head_dim = queries.shape
    key_all = jnp.concatenate([tail_k, keys], axis=0)
    value_all = jnp.concatenate([tail_v, values], axis=0)
    scores = lax.dot_general(
        queries, key_all, (((1,), (1,)), ((), ())), preferred_element_type=f32
    ) * head_dim ** (-0.5)
    query_pos = jnp.arange(tok_rows, dtype=jnp.int32)[:, None]
    key_pos = jnp.arange(tok_rows + WIN, dtype=jnp.int32)[None, :] - WIN
    in_window = (
        (key_pos <= query_pos)
        & (key_pos > query_pos - WIN)
        & (key_pos + seq_index * tok_rows >= 0)
    )
    scores = jnp.where(in_window, scores, -1e30)
    row_max = jnp.max(scores, axis=-1, keepdims=True)
    expo = jnp.exp(scores - row_max)
    probs = (expo / jnp.sum(expo, axis=-1, keepdims=True)).astype(bf16)
    return jnp.dot(probs, value_all, preferred_element_type=f32)


def renorm(weights, updated):
    target = jnp.sqrt(jnp.mean(weights * weights, axis=-1, keepdims=True))
    return updated * (
        target / jnp.sqrt(jnp.mean(updated * updated, axis=-1, keepdims=True) + 1e-06)
    )


def adam_step(weights, gradient, first_moment, second_moment):
    first_next = beta_one * first_moment + (1.0 - beta_one) * gradient
    second_next = beta_two * second_moment + (1.0 - beta_two) * gradient * gradient
    first_hat = first_next / (1.0 - beta_one**10)
    second_hat = second_next / (1.0 - beta_two**10)
    return (
        weights - adam_rate * first_hat / (jnp.sqrt(second_hat) + 1e-08),
        first_next,
        second_next,
    )


def inner_local(queries, keys, values, rates, gain, cotangent, fast_init, first_moment, second_moment):
    tokens, dim = queries.shape
    zh = lax.axis_index("zh")
    plane = lax.axis_index(PLANE)
    weights = fast_init[0]
    half = ((tokens, dim), bf16)
    full, far = pltpu.VMEM((tokens, dim), f32), jax.ShapeDtypeStruct((tokens, dim), f32)
    side = ((tokens, 128), f32)
    mats = ((3, dim, dim), bf16)
    owned = pltpu.VMEM((NP, NH * 3 * ROWS, dim), bf16)
    gain_row = gain[None, :]

    last = NY * NP - 1
    pairs = [(i, i + 1) for i in range(last)]
    tails = jnp.stack([keys[tokens - WIN :], values[tokens - WIN :]])
    tails = lax.ppermute(tails, SEQ, pairs)

    parts, first_pre, third_pre, back = called(
        inner_kernel, [owned, far, far, far], [mats, side, half, half, half],
        keys, values, rates, weights,
    )
    init_rows = lax.dynamic_slice_in_dim(weights, (zh * NP + plane) * ROWS, ROWS, 1)
    moved_rows = init_rows - reduce_rows(parts)
    renormed = gather_rows(renorm(init_rows, moved_rows).astype(bf16))

    fast_out, first_q, third_q, sums, second_w = called(
        forward_kernel, [full, full, full, pltpu.VMEM((NP, 2, tokens), f32), pltpu.VMEM(*half)], [mats, side],
        near(renormed), queries, cotangent, gain_row,
    )
    sums = swapped(sums, HEAD)
    parts, normed = called(
        backward_kernel, [owned, far], [((2, tokens, 128), f32), half, half, half, half],
        near(sums), near(fast_out), near(first_q), near(third_q), queries, cotangent, gain_row,
        near(second_w),
    )
    cot_rows = reduce_rows(parts)
    _, pull_norm = jax.vjp(renorm, init_rows, moved_rows)
    d_init_rows, d_moved_rows = pull_norm(cot_rows)
    direction = gather_rows(d_moved_rows.astype(bf16))

    (parts,) = called(
        second_kernel, [owned], [mats, side, half, half, half],
        near(direction), keys, values, rates, first_pre, third_pre, back,
    )
    grad_rows = d_init_rows + d_moved_rows - reduce_rows(parts)
    attention = attention_of(
        queries, keys, values, tails[0], tails[1], zh * NP + plane
    )
    layer_out = (attention + normed).astype(bf16)
    new = adam_step(init_rows, grad_rows, first_moment[0], second_moment[0])
    return (layer_out, new[0][None], new[1][None], new[2][None])


def solution(mesh):
    split = Mesh(mesh.devices.reshape(NH, 2, NY, 4, 2), ("zh", "zl", "y", "x", "c"))
    placed = (
        P(SEQ, HEAD),
        P(SEQ, HEAD),
        P(SEQ, HEAD),
        P(HEAD, SEQ),
        P(HEAD),
        P(SEQ, HEAD),
        P(HEAD, None, None, None),
        P(HEAD, None, SEQ, None),
        P(HEAD, None, SEQ, None),
    )
    return jax.shard_map(
        inner_local,
        mesh=split,
        in_specs=placed,
        out_specs=(
            P(SEQ, HEAD),
            P(HEAD, None, SEQ, None),
            P(HEAD, None, SEQ, None),
            P(HEAD, None, SEQ, None),
        ),
        check_vma=False,
    )
```

```python
import jax
import jax.numpy as jnp
from jax import lax
from jax.experimental import pallas as pl
from jax.experimental.pallas import tpu as pltpu
from jax.sharding import Mesh
from jax.sharding import PartitionSpec as P


WIN = 256
WIDTH = 4096
SEQ = ("zh", "zl", "y")
PLANE = ("zl", "y")
HEAD = ("x", "c")
NY = 4
NH = 4
NP = 8
ROWS = 16
BLOCK = 128
VMEM_BYTES = 24 * 1024 * 1024
beta_one = 0.9
beta_two = 0.95
adam_rate = 0.02
bf16 = jnp.bfloat16
f32 = jnp.float32


def mm(a, b, ca, cb):
    return lax.dot_general(
        a.astype(bf16), b.astype(bf16), (((ca,), (cb,)), ((), ())), preferred_element_type=f32
    )


def swapped(parts, axes):
    return lax.all_to_all(parts, axes, split_axis=0, concat_axis=0, tiled=True)


def copies(array, count):
    return jnp.broadcast_to(array, (count, *array.shape))


def totals(parts):
    return jnp.sum(parts.astype(f32), axis=0)


def gates(pre):
    sig = 1.0 / (1.0 + jnp.exp(-pre))
    d_sig = sig * (1.0 - sig)
    return pre * sig, sig + pre * d_sig, d_sig * (2.0 + pre * (1.0 - 2.0 * sig))


def columns(row):
    return jnp.broadcast_to(row, (128, row.shape[1])).T


def blocks_of(count, body):
    def step(j, carry):
        body(pl.ds(pl.multiple_of(j * BLOCK, BLOCK), BLOCK))
        return carry

    lax.fori_loop(0, count // BLOCK, step, 0)


def put_grad(parts_ref, number, left, right):
    grad = mm(left[...], right[...], 0, 0).astype(bf16)
    for m in range(grad.shape[0] // ROWS):
        at = (m // NP * 3 + number) * ROWS
        parts_ref[m % NP, at : at + ROWS, :] = grad[m * ROWS : (m + 1) * ROWS]


def take_matrices(parts_ref, out_ref):
    for number in range(out_ref.shape[0]):
        for m in range(out_ref.shape[1] // ROWS):
            at = (m // NP * 3 + number) * ROWS
            out_ref[number, m * ROWS : (m + 1) * ROWS, :] = parts_ref[m % NP, at : at + ROWS, :]


def inner_kernel(
    seq_ref, k_ref, v_ref, r_ref, w_ref,
    parts_ref, p1_ref, p3_ref, b_ref, own_ref, w_s, f_s, d1, d3, d2,
):
    tokens, dim = k_ref.shape
    scale = dim ** (-0.5)
    own = pl.ds(pl.multiple_of(seq_ref[0] * ROWS, ROWS), ROWS)
    for m in range(3):
        w_s[m] = w_ref[m].astype(bf16)
        own_ref[m * ROWS : (m + 1) * ROWS, :] = w_ref[m, own, :]
    f_s[...] = columns(r_ref[...] * (-scale))

    def body(at):
        factor = f_s[at, :][:, :1]
        p1 = scale * mm(k_ref[at, :], w_s[0], 1, 0)
        p3 = scale * mm(k_ref[at, :], w_s[1], 1, 0)
        back = factor * mm(v_ref[at, :], w_s[2], 1, 0)
        gate, gate1, _ = gates(p1)
        p1_ref[at, :] = p1
        p3_ref[at, :] = p3
        b_ref[at, :] = back
        d1[at, :] = (scale * back * p3 * gate1).astype(bf16)
        d3[at, :] = (scale * back * gate).astype(bf16)
        d2[at, :] = (factor * gate * p3).astype(bf16)

    blocks_of(tokens, body)
    put_grad(parts_ref, 0, k_ref, d1)
    put_grad(parts_ref, 1, k_ref, d3)
    put_grad(parts_ref, 2, v_ref, d2)


def forward_kernel(got_ref, q_ref, cot_ref, gain_ref, o_ref, p1_ref, p3_ref, sums_ref, w2_ref, w_s, s_s):
    tokens, dim = q_ref.shape
    scale = dim ** (-0.5)
    take_matrices(got_ref, w_s)
    w2_ref[...] = w_s[2]

    def body(at):
        p1 = scale * mm(q_ref[at, :], w_s[0], 1, 0)
        p3 = scale * mm(q_ref[at, :], w_s[1], 1, 0)
        gate, _, _ = gates(p1)
        out = scale * mm(gate * p3, w_s[2], 1, 1)
        p1_ref[at, :] = p1
        p3_ref[at, :] = p3
        o_ref[at, :] = out
        weighted = cot_ref[at, :].astype(f32) * gain_ref[...]
        squares = jnp.sum(out * out, axis=1, keepdims=True)
        inner = jnp.sum(weighted * out, axis=1, keepdims=True)
        lane = lax.broadcasted_iota(jnp.int32, (BLOCK, 128), 1)
        s_s[at, :] = jnp.where(lane == 0, squares, inner)

    blocks_of(tokens, body)
    sums_ref[...] = jnp.broadcast_to(s_s[...].T[:2, :], sums_ref.shape)


def backward_kernel(
    seq_ref, sums_ref, o_ref, p1_ref, p3_ref, q_ref, cot_ref, gain_ref, w2_ref, k_ref, v_ref, tails_ref,
    parts_ref, layer_ref, s_s, d1, d3, a_s, e_s, all_s,
):
    tokens, dim = q_ref.shape
    scale = dim ** (-0.5)
    all_s[:, :WIN, :] = tails_ref[...]
    all_s[0, WIN:, :] = k_ref[...]
    all_s[1, WIN:, :] = v_ref[...]
    span = BLOCK + WIN
    ahead = lax.broadcasted_iota(jnp.int32, (BLOCK, span), 1)
    behind = ahead - lax.broadcasted_iota(jnp.int32, (BLOCK, span), 0)
    near_by = (behind > 0) & (behind <= WIN)
    sums = jnp.sum(sums_ref[...], axis=0)
    inverse = 1.0 / jnp.sqrt(sums[:1] / WIDTH + 1e-06)
    coef = sums[1:] * inverse * inverse * inverse / WIDTH
    s_s[0] = columns(inverse)
    s_s[1] = columns(coef)

    def body(at):
        inv = s_s[0, at, :][:, :1]
        out = o_ref[at, :]
        weighted = cot_ref[at, :].astype(f32) * gain_ref[...]
        err = (scale * (weighted * inv - out * s_s[1, at, :][:, :1])).astype(bf16)
        e_s[at, :] = err
        window = pl.ds(at.start, span)
        scores = scale * mm(q_ref[at, :], all_s[0, window, :], 1, 1)
        known = near_by & (ahead + (seq_ref[0] * tokens + at.start) >= WIN)
        scores = jnp.where(known, scores, -1e30)
        expo = jnp.exp(scores - jnp.max(scores, axis=1, keepdims=True))
        probs = expo / jnp.sum(expo, axis=1, keepdims=True)
        attention = mm(probs, all_s[1, window, :], 1, 0)
        layer_ref[at, :] = (attention + out * inv * gain_ref[...]).astype(bf16)
        back = mm(err, w2_ref[...], 1, 0)
        p3 = p3_ref[at, :]
        gate, gate1, _ = gates(p1_ref[at, :])
        d1[at, :] = (scale * back * p3 * gate1).astype(bf16)
        d3[at, :] = (scale * back * gate).astype(bf16)
        a_s[at, :] = (gate * p3).astype(bf16)

    blocks_of(tokens, body)
    put_grad(parts_ref, 0, q_ref, d1)
    put_grad(parts_ref, 1, q_ref, d3)
    put_grad(parts_ref, 2, e_s, a_s)


def second_kernel(got_ref, k_ref, v_ref, r_ref, p1_ref, p3_ref, b_ref, parts_ref, w_s, f_s, d1, d3, d2):
    tokens, dim = k_ref.shape
    scale = dim ** (-0.5)
    take_matrices(got_ref, w_s)
    f_s[...] = columns(r_ref[...] * (-scale))

    def body(at):
        factor = f_s[at, :][:, :1]
        first_dot = scale * mm(k_ref[at, :], w_s[0], 1, 0)
        third_dot = scale * mm(k_ref[at, :], w_s[1], 1, 0)
        back_dot = factor * mm(v_ref[at, :], w_s[2], 1, 0)
        p3 = p3_ref[at, :]
        back = b_ref[at, :]
        gate, gate1, gate2 = gates(p1_ref[at, :])
        bent = gate1 * first_dot
        d1[at, :] = (
            scale
            * (gate1 * (back_dot * p3 + back * third_dot) + back * p3 * gate2 * first_dot)
        ).astype(bf16)
        d3[at, :] = (scale * (back_dot * gate + back * bent)).astype(bf16)
        d2[at, :] = (factor * (bent * p3 + gate * third_dot)).astype(bf16)

    blocks_of(tokens, body)
    put_grad(parts_ref, 0, k_ref, d1)
    put_grad(parts_ref, 1, k_ref, d3)
    put_grad(parts_ref, 2, v_ref, d2)


def near(array):
    return pltpu.with_memory_space_constraint(array, pltpu.VMEM)


def total_kernel(got_ref, out_ref):
    peers, height, _ = out_ref.shape
    for m in range(peers):
        out_ref[m] = totals(got_ref[:, m * height : (m + 1) * height, :]).astype(bf16)


def means(array):
    return jnp.mean(array, axis=1, keepdims=True)


def moved_kernel(got_ref, own_ref, moved_ref, out_ref):
    own = own_ref[...]
    moved = own - totals(got_ref[...])
    moved_ref[...] = moved
    factor = jnp.sqrt(means(own * own)) / jnp.sqrt(means(moved * moved) + 1e-06)
    out_ref[...] = copies((moved * factor).astype(bf16), NH)


def pulled_kernel(got_ref, own_ref, moved_ref, part_ref, out_ref):
    own, moved = own_ref[...], moved_ref[...]
    cot = totals(got_ref[...])
    target = jnp.sqrt(means(own * own))
    inverse = 1.0 / jnp.sqrt(means(moved * moved) + 1e-06)
    along = means(cot * moved) * inverse
    d_moved = (target * inverse) * (cot - moved * (along * inverse))
    part_ref[...] = d_moved + own * (along / target)
    out_ref[...] = copies(d_moved.astype(bf16), NH)


def called(kernel, outs, scratch, *args):
    return pl.pallas_call(
        kernel,
        out_shape=outs,
        in_specs=[
            pl.BlockSpec(memory_space=pltpu.SMEM if arg.dtype == jnp.int32 else pltpu.VMEM)
            for arg in args
        ],
        out_specs=[pl.BlockSpec(memory_space=pltpu.VMEM)] * len(outs),
        scratch_shapes=[pltpu.VMEM(*item) for item in scratch],
        compiler_params=pltpu.CompilerParams(vmem_limit_bytes=VMEM_BYTES),
    )(*args)


def reduce_rows(parts):
    some = swapped(parts, PLANE)
    shape = (NH, parts.shape[1] // NH, parts.shape[2])
    (some,) = called(total_kernel, [pltpu.VMEM(shape, bf16)], [], near(some))
    return swapped(some, "zh")


def gather_rows(rows):
    some = swapped(rows, "zh")
    return swapped(copies(some.reshape(-1, rows.shape[2]), NP), PLANE)


def adam_step(weights, gradient, first_moment, second_moment):
    first_next = beta_one * first_moment + (1.0 - beta_one) * gradient
    second_next = beta_two * second_moment + (1.0 - beta_two) * gradient * gradient
    first_hat = first_next / (1.0 - beta_one**10)
    second_hat = second_next / (1.0 - beta_two**10)
    return (
        weights - adam_rate * first_hat / (jnp.sqrt(second_hat) + 1e-08),
        first_next,
        second_next,
    )


def inner_local(queries, keys, values, rates, gain, cotangent, fast_init, first_moment, second_moment):
    tokens, dim = queries.shape
    seq = lax.axis_index(SEQ).astype(jnp.int32).reshape(1)
    half = ((tokens, dim), bf16)
    full = pltpu.VMEM((tokens, dim), f32)
    far = jax.ShapeDtypeStruct((tokens, dim), f32)
    side = ((tokens, 128), f32)
    mats = ((3, dim, dim), bf16)
    owned = pltpu.VMEM((NP, NH * 3 * ROWS, dim), bf16)
    rows = pltpu.VMEM((3 * ROWS, dim), f32)
    alike = pltpu.VMEM((NH, 3 * ROWS, dim), bf16)
    gain_row = gain[None, :]

    last = NY * NP - 1
    pairs = [(i, i + 1) for i in range(last)]
    tails = jnp.stack([keys[tokens - WIN :], values[tokens - WIN :]])
    tails = lax.ppermute(tails, SEQ, pairs)

    parts, first_pre, third_pre, back, own = called(
        inner_kernel, [owned, far, far, far, rows], [mats, side, half, half, half],
        seq, keys, values, rates, fast_init[0],
    )
    got = reduce_rows(parts)
    moved, out = called(moved_kernel, [rows, alike], [], near(got), near(own))
    renormed = gather_rows(out)

    fast_out, first_q, third_q, sums, second_w = called(
        forward_kernel,
        [full, full, full, pltpu.VMEM((NP, 2, tokens), f32), pltpu.VMEM(*half)], [mats, side],
        near(renormed), queries, cotangent, gain_row,
    )
    sums = swapped(sums, HEAD)
    parts, layer_out = called(
        backward_kernel, [owned, jax.ShapeDtypeStruct(*half)],
        [((2, tokens, 128), f32), half, half, half, half, ((2, tokens + WIN, dim), bf16)],
        seq, near(sums), near(fast_out), near(first_q), near(third_q), queries, cotangent, gain_row,
        near(second_w), keys, values, tails,
    )
    got = reduce_rows(parts)
    part, out = called(pulled_kernel, [rows, alike], [], near(got), near(own), near(moved))
    direction = gather_rows(out)

    (parts,) = called(
        second_kernel, [owned], [mats, side, half, half, half],
        near(direction), keys, values, rates, first_pre, third_pre, back,
    )
    grad_rows = part - totals(reduce_rows(parts))
    shape = first_moment[0].shape
    new = adam_step(own.reshape(shape), grad_rows.reshape(shape), first_moment[0], second_moment[0])
    return (layer_out, new[0][None], new[1][None], new[2][None])


def solution(mesh):
    split = Mesh(mesh.devices.reshape(NH, 2, NY, 4, 2), ("zh", "zl", "y", "x", "c"))
    placed = (
        P(SEQ, HEAD),
        P(SEQ, HEAD),
        P(SEQ, HEAD),
        P(HEAD, SEQ),
        P(HEAD),
        P(SEQ, HEAD),
        P(HEAD, None, None, None),
        P(HEAD, None, SEQ, None),
        P(HEAD, None, SEQ, None),
    )
    return jax.shard_map(
        inner_local,
        mesh=split,
        in_specs=placed,
        out_specs=(
            P(SEQ, HEAD),
            P(HEAD, None, SEQ, None),
            P(HEAD, None, SEQ, None),
            P(HEAD, None, SEQ, None),
        ),
        check_vma=False,
    )
```

```python
import jax
import jax.numpy as jnp
from jax import lax
from jax.experimental import pallas as pl
from jax.experimental.pallas import tpu as pltpu
from jax.sharding import Mesh
from jax.sharding import PartitionSpec as P


WIN = 256
WIDTH = 4096
SEQ = ("zh", "zl", "y")
PLANE = ("zl", "y")
HEAD = ("x", "c")
NY = 4
NH = 4
NP = 8
ROWS = 16
BLOCK = 128
VMEM_BYTES = 24 * 1024 * 1024
beta_one = 0.9
beta_two = 0.95
adam_rate = 0.02
bf16 = jnp.bfloat16
f32 = jnp.float32


def mm(a, b, ca, cb):
    return lax.dot_general(
        a.astype(bf16), b.astype(bf16), (((ca,), (cb,)), ((), ())), preferred_element_type=f32
    )


def swapped(parts, axes):
    return lax.all_to_all(parts, axes, split_axis=0, concat_axis=0, tiled=True)


def copies(array, count):
    return jnp.broadcast_to(array, (count, *array.shape))


def totals(parts):
    return jnp.sum(parts.astype(f32), axis=0)


def gates(pre):
    sig = 1.0 / (1.0 + jnp.exp(-pre))
    d_sig = sig * (1.0 - sig)
    return pre * sig, sig + pre * d_sig, d_sig * (2.0 + pre * (1.0 - 2.0 * sig))


def columns(row):
    return jnp.broadcast_to(row, (128, row.shape[1])).T


def blocks_of(count, body):
    def step(j, carry):
        body(pl.ds(pl.multiple_of(j * BLOCK, BLOCK), BLOCK))
        return carry

    lax.fori_loop(0, count // BLOCK, step, 0)


def put_grad(parts_ref, number, left, right):
    grad = mm(left[...], right[...], 0, 0).astype(bf16)
    for m in range(grad.shape[0] // ROWS):
        at = (m // NP * 3 + number) * ROWS
        parts_ref[m % NP, at : at + ROWS, :] = grad[m * ROWS : (m + 1) * ROWS]


def take_matrices(parts_ref, out_ref):
    for number in range(out_ref.shape[0]):
        for m in range(out_ref.shape[1] // ROWS):
            at = (m // NP * 3 + number) * ROWS
            out_ref[number, m * ROWS : (m + 1) * ROWS, :] = parts_ref[m % NP, at : at + ROWS, :]


def inner_kernel(
    seq_ref, k_hbm, v_hbm, r_hbm, w_hbm,
    parts_ref, p1_ref, p3_ref, b_ref, own_ref, tails_ref, f_s,
    w_s, d1, d3, d2, k_ref, v_ref, r_ref, w_ref, sems,
):
    inputs = ((k_hbm, k_ref), (w_hbm, w_ref), (r_hbm, r_ref), (v_hbm, v_ref))
    fetches = [
        pltpu.make_async_copy(source, target, sems.at[number])
        for number, (source, target) in enumerate(inputs)
    ]
    for fetch in fetches:
        fetch.start()
    for fetch in fetches:
        fetch.wait()
    tokens, dim = k_ref.shape
    tails_ref[0] = k_ref[tokens - WIN :, :]
    tails_ref[1] = v_ref[tokens - WIN :, :]
    scale = dim ** (-0.5)
    own = pl.ds(pl.multiple_of(seq_ref[0] * ROWS, ROWS), ROWS)
    for m in range(3):
        w_s[m] = w_ref[m].astype(bf16)
        own_ref[m * ROWS : (m + 1) * ROWS, :] = w_ref[m, own, :]
    f_s[...] = columns(r_ref[...] * (-scale))

    def body(at):
        factor = f_s[at, :][:, :1]
        p1 = scale * mm(k_ref[at, :], w_s[0], 1, 0)
        p3 = scale * mm(k_ref[at, :], w_s[1], 1, 0)
        back = factor * mm(v_ref[at, :], w_s[2], 1, 0)
        gate, gate1, _ = gates(p1)
        p1_ref[at, :] = p1
        p3_ref[at, :] = p3
        b_ref[at, :] = back
        d1[at, :] = (scale * back * p3 * gate1).astype(bf16)
        d3[at, :] = (scale * back * gate).astype(bf16)
        d2[at, :] = (factor * gate * p3).astype(bf16)

    blocks_of(tokens, body)
    put_grad(parts_ref, 0, k_ref, d1)
    put_grad(parts_ref, 1, k_ref, d3)
    put_grad(parts_ref, 2, v_ref, d2)


def forward_kernel(got_ref, q_ref, cot_ref, gain_ref, o_ref, p1_ref, p3_ref, sums_ref, w2_ref, w_s, s_s):
    tokens, dim = q_ref.shape
    scale = dim ** (-0.5)
    take_matrices(got_ref, w_s)
    w2_ref[...] = w_s[2]

    def body(at):
        p1 = scale * mm(q_ref[at, :], w_s[0], 1, 0)
        p3 = scale * mm(q_ref[at, :], w_s[1], 1, 0)
        gate, _, _ = gates(p1)
        out = scale * mm(gate * p3, w_s[2], 1, 1)
        p1_ref[at, :] = p1
        p3_ref[at, :] = p3
        o_ref[at, :] = out
        weighted = cot_ref[at, :].astype(f32) * gain_ref[...]
        squares = jnp.sum(out * out, axis=1, keepdims=True)
        inner = jnp.sum(weighted * out, axis=1, keepdims=True)
        lane = lax.broadcasted_iota(jnp.int32, (BLOCK, 128), 1)
        s_s[at, :] = jnp.where(lane == 0, squares, inner)

    blocks_of(tokens, body)
    sums_ref[...] = jnp.broadcast_to(s_s[...].T[:2, :], sums_ref.shape)


def backward_kernel(
    seq_ref, sums_ref, o_ref, p1_ref, p3_ref, q_ref, cot_ref, gain_ref, w2_ref, k_ref, v_ref, tails_ref,
    parts_ref, layer_ref, s_s, d1, d3, a_s, e_s, all_s,
):
    tokens, dim = q_ref.shape
    scale = dim ** (-0.5)
    all_s[:, :WIN, :] = tails_ref[...]
    all_s[0, WIN:, :] = k_ref[...]
    all_s[1, WIN:, :] = v_ref[...]
    span = BLOCK + WIN
    ahead = lax.broadcasted_iota(jnp.int32, (BLOCK, span), 1)
    behind = ahead - lax.broadcasted_iota(jnp.int32, (BLOCK, span), 0)
    near_by = (behind > 0) & (behind <= WIN)
    sums = jnp.sum(sums_ref[...], axis=0)
    inverse = 1.0 / jnp.sqrt(sums[:1] / WIDTH + 1e-06)
    coef = sums[1:] * inverse * inverse * inverse / WIDTH
    s_s[0] = columns(inverse)
    s_s[1] = columns(coef)

    def body(at):
        inv = s_s[0, at, :][:, :1]
        out = o_ref[at, :]
        weighted = cot_ref[at, :].astype(f32) * gain_ref[...]
        err = (scale * (weighted * inv - out * s_s[1, at, :][:, :1])).astype(bf16)
        e_s[at, :] = err
        window = pl.ds(at.start, span)
        scores = scale * mm(q_ref[at, :], all_s[0, window, :], 1, 1)
        known = near_by & (ahead + (seq_ref[0] * tokens + at.start) >= WIN)
        scores = jnp.where(known, scores, -1e30)
        expo = jnp.exp(scores - jnp.max(scores, axis=1, keepdims=True))
        probs = expo / jnp.sum(expo, axis=1, keepdims=True)
        attention = mm(probs, all_s[1, window, :], 1, 0)
        layer_ref[at, :] = (attention + out * inv * gain_ref[...]).astype(bf16)
        back = mm(err, w2_ref[...], 1, 0)
        p3 = p3_ref[at, :]
        gate, gate1, _ = gates(p1_ref[at, :])
        d1[at, :] = (scale * back * p3 * gate1).astype(bf16)
        d3[at, :] = (scale * back * gate).astype(bf16)
        a_s[at, :] = (gate * p3).astype(bf16)

    blocks_of(tokens, body)
    put_grad(parts_ref, 0, q_ref, d1)
    put_grad(parts_ref, 1, q_ref, d3)
    put_grad(parts_ref, 2, e_s, a_s)


def second_kernel(got_ref, k_ref, v_ref, f_s, p1_ref, p3_ref, b_ref, parts_ref, w_s, d1, d3, d2):
    tokens, dim = k_ref.shape
    scale = dim ** (-0.5)
    take_matrices(got_ref, w_s)

    def body(at):
        factor = f_s[at, :][:, :1]
        first_dot = scale * mm(k_ref[at, :], w_s[0], 1, 0)
        third_dot = scale * mm(k_ref[at, :], w_s[1], 1, 0)
        back_dot = factor * mm(v_ref[at, :], w_s[2], 1, 0)
        p3 = p3_ref[at, :]
        back = b_ref[at, :]
        gate, gate1, gate2 = gates(p1_ref[at, :])
        bent = gate1 * first_dot
        d1[at, :] = (
            scale
            * (gate1 * (back_dot * p3 + back * third_dot) + back * p3 * gate2 * first_dot)
        ).astype(bf16)
        d3[at, :] = (scale * (back_dot * gate + back * bent)).astype(bf16)
        d2[at, :] = (factor * (bent * p3 + gate * third_dot)).astype(bf16)

    blocks_of(tokens, body)
    put_grad(parts_ref, 0, k_ref, d1)
    put_grad(parts_ref, 1, k_ref, d3)
    put_grad(parts_ref, 2, v_ref, d2)


def near(array):
    return pltpu.with_memory_space_constraint(array, pltpu.VMEM)


def total_kernel(got_ref, out_ref):
    peers, height, _ = out_ref.shape
    for m in range(peers):
        out_ref[m] = totals(got_ref[:, m * height : (m + 1) * height, :]).astype(bf16)


def means(array):
    return jnp.mean(array, axis=1, keepdims=True)


def moved_kernel(got_ref, own_ref, moved_ref, out_ref):
    own = own_ref[...]
    moved = own - totals(got_ref[...])
    moved_ref[...] = moved
    factor = jnp.sqrt(means(own * own)) / jnp.sqrt(means(moved * moved) + 1e-06)
    out_ref[...] = copies((moved * factor).astype(bf16), NH)


def pulled_kernel(got_ref, own_ref, moved_ref, part_ref, out_ref):
    own, moved = own_ref[...], moved_ref[...]
    cot = totals(got_ref[...])
    target = jnp.sqrt(means(own * own))
    inverse = 1.0 / jnp.sqrt(means(moved * moved) + 1e-06)
    along = means(cot * moved) * inverse
    d_moved = (target * inverse) * (cot - moved * (along * inverse))
    part_ref[...] = d_moved + own * (along / target)
    out_ref[...] = copies(d_moved.astype(bf16), NH)


def place(arg, inputs_stay):
    if arg.dtype == jnp.int32:
        return pl.BlockSpec(memory_space=pltpu.SMEM)
    return pl.BlockSpec(memory_space=pltpu.HBM if inputs_stay else pltpu.VMEM)


def called(kernel, outs, scratch, *args, inputs_stay=False):
    return pl.pallas_call(
        kernel,
        out_shape=outs,
        in_specs=[place(arg, inputs_stay) for arg in args],
        out_specs=[pl.BlockSpec(memory_space=pltpu.VMEM)] * len(outs),
        scratch_shapes=[pltpu.VMEM(*item) if isinstance(item, tuple) else item for item in scratch],
        compiler_params=pltpu.CompilerParams(vmem_limit_bytes=VMEM_BYTES),
    )(*args)


def reduce_rows(parts):
    some = swapped(parts, PLANE)
    shape = (NH, parts.shape[1] // NH, parts.shape[2])
    (some,) = called(total_kernel, [pltpu.VMEM(shape, bf16)], [], near(some))
    return swapped(some, "zh")


def gather_rows(rows):
    some = swapped(rows, "zh")
    return swapped(copies(some.reshape(-1, rows.shape[2]), NP), PLANE)


def adam_step(weights, gradient, first_moment, second_moment):
    first_next = beta_one * first_moment + (1.0 - beta_one) * gradient
    second_next = beta_two * second_moment + (1.0 - beta_two) * gradient * gradient
    first_hat = first_next / (1.0 - beta_one**10)
    second_hat = second_next / (1.0 - beta_two**10)
    return (
        weights - adam_rate * first_hat / (jnp.sqrt(second_hat) + 1e-08),
        first_next,
        second_next,
    )


def inner_local(queries, keys, values, rates, gain, cotangent, fast_init, first_moment, second_moment):
    tokens, dim = queries.shape
    seq = lax.axis_index(SEQ).astype(jnp.int32).reshape(1)
    half = ((tokens, dim), bf16)
    full = pltpu.VMEM((tokens, dim), f32)
    far = jax.ShapeDtypeStruct((tokens, dim), f32)
    side = ((tokens, 128), f32)
    mats = ((3, dim, dim), bf16)
    owned = pltpu.VMEM((NP, NH * 3 * ROWS, dim), bf16)
    rows = pltpu.VMEM((3 * ROWS, dim), f32)
    alike = pltpu.VMEM((NH, 3 * ROWS, dim), bf16)
    gain_row = gain[None, :]

    parts, first_pre, third_pre, back, own, tails, factors = called(
        inner_kernel, [owned, far, far, far, rows, pltpu.VMEM((2, WIN, dim), bf16), pltpu.VMEM(*side)],
        [mats, half, half, half, half, half, ((1, tokens), f32), (mats[0], f32),
         pltpu.SemaphoreType.DMA((4,))],
        seq, *(pltpu.with_memory_space_constraint(a, pltpu.HBM) for a in (keys, values, rates, fast_init[0])),
        inputs_stay=True,
    )
    last = NY * NP - 1
    tails = lax.ppermute(tails, SEQ, [(i, i + 1) for i in range(last)])
    got = reduce_rows(parts)
    moved, out = called(moved_kernel, [rows, alike], [], near(got), near(own))
    renormed = gather_rows(out)

    fast_out, first_q, third_q, sums, second_w = called(
        forward_kernel,
        [full, full, full, pltpu.VMEM((NP, 2, tokens), f32), pltpu.VMEM(*half)], [mats, side],
        near(renormed), queries, cotangent, gain_row,
    )
    sums = swapped(sums, HEAD)
    parts, layer_out = called(
        backward_kernel, [owned, jax.ShapeDtypeStruct(*half)],
        [((2, tokens, 128), f32), half, half, half, half, ((2, tokens + WIN, dim), bf16)],
        seq, near(sums), near(fast_out), near(first_q), near(third_q), queries, cotangent, gain_row,
        near(second_w), keys, values, tails,
    )
    got = reduce_rows(parts)
    part, out = called(pulled_kernel, [rows, alike], [], near(got), near(own), near(moved))
    direction = gather_rows(out)

    (parts,) = called(
        second_kernel, [owned], [mats, half, half, half],
        near(direction), keys, values, near(factors), first_pre, third_pre, back,
    )
    grad_rows = part - totals(reduce_rows(parts))
    shape = first_moment[0].shape
    new = adam_step(own.reshape(shape), grad_rows.reshape(shape), first_moment[0], second_moment[0])
    return (layer_out, new[0][None], new[1][None], new[2][None])


def solution(mesh):
    split = Mesh(mesh.devices.reshape(NH, 2, NY, 4, 2), ("zh", "zl", "y", "x", "c"))
    placed = (
        P(SEQ, HEAD),
        P(SEQ, HEAD),
        P(SEQ, HEAD),
        P(HEAD, SEQ),
        P(HEAD),
        P(SEQ, HEAD),
        P(HEAD, None, None, None),
        P(HEAD, None, SEQ, None),
        P(HEAD, None, SEQ, None),
    )
    return jax.shard_map(
        inner_local,
        mesh=split,
        in_specs=placed,
        out_specs=(
            P(SEQ, HEAD),
            P(HEAD, None, SEQ, None),
            P(HEAD, None, SEQ, None),
            P(HEAD, None, SEQ, None),
        ),
        check_vma=False,
    )
```

```python
import jax
import jax.numpy as jnp
from jax import lax
from jax.experimental import pallas as pl
from jax.experimental.pallas import tpu as pltpu
from jax.sharding import Mesh
from jax.sharding import PartitionSpec as P


WIN = 256
WIDTH = 4096
SEQ = ("zh", "zl", "y")
PLANE = ("zl", "y")
HEAD = ("x", "c")
NY = 4
NH = 4
NP = 8
ROWS = 16
BLOCK = 128
VMEM_BYTES = 24 * 1024 * 1024
beta_one = 0.9
beta_two = 0.95
adam_rate = 0.02
bf16 = jnp.bfloat16
f32 = jnp.float32


def mm(a, b, ca, cb):
    return lax.dot_general(
        a.astype(bf16), b.astype(bf16), (((ca,), (cb,)), ((), ())), preferred_element_type=f32
    )


def swapped(parts, axes):
    return lax.all_to_all(parts, axes, split_axis=0, concat_axis=0, tiled=True)


def copies(array, count):
    return jnp.broadcast_to(array, (count, *array.shape))


def totals(parts):
    return jnp.sum(parts.astype(f32), axis=0)


def gates(pre):
    sig = 1.0 / (1.0 + jnp.exp(-pre))
    d_sig = sig * (1.0 - sig)
    return pre * sig, sig + pre * d_sig, d_sig * (2.0 + pre * (1.0 - 2.0 * sig))


def columns(row):
    return jnp.broadcast_to(row, (128, row.shape[1])).T


def blocks_of(count, body):
    def step(j, carry):
        body(pl.ds(pl.multiple_of(j * BLOCK, BLOCK), BLOCK))
        return carry

    lax.fori_loop(0, count // BLOCK, step, 0)


def put_grad(parts_ref, number, left, right):
    grad = mm(left[...], right[...], 0, 0).astype(bf16)
    for m in range(grad.shape[0] // ROWS):
        at = (m // NP * 3 + number) * ROWS
        parts_ref[m % NP, at : at + ROWS, :] = grad[m * ROWS : (m + 1) * ROWS]


def take_matrices(parts_ref, out_ref):
    for number in range(out_ref.shape[0]):
        for m in range(out_ref.shape[1] // ROWS):
            at = (m // NP * 3 + number) * ROWS
            out_ref[number, m * ROWS : (m + 1) * ROWS, :] = parts_ref[m % NP, at : at + ROWS, :]


def inner_kernel(
    seq_ref, k_hbm, v_hbm, r_hbm, w_hbm,
    parts_ref, p1_ref, p3_ref, b_ref, own_ref, tails_ref, f_s,
    w_s, d1, d3, d2, k_ref, v_ref, r_ref, w_ref, sems,
):
    inputs = [(k_hbm, k_ref)] + [(w_hbm.at[m], w_ref.at[m]) for m in range(3)]
    inputs += [(v_hbm, v_ref), (r_hbm, r_ref)]
    fetches = [
        pltpu.make_async_copy(source, target, sems.at[number])
        for number, (source, target) in enumerate(inputs)
    ]
    for fetch in fetches:
        fetch.start()
    tokens, dim = k_ref.shape
    scale = dim ** (-0.5)
    for fetch in fetches[:3]:
        fetch.wait()
    w_s[0] = w_ref[0].astype(bf16)
    w_s[1] = w_ref[1].astype(bf16)

    def first(at):
        p1_ref[at, :] = scale * mm(k_ref[at, :], w_s[0], 1, 0)
        p3_ref[at, :] = scale * mm(k_ref[at, :], w_s[1], 1, 0)

    blocks_of(tokens, first)
    for fetch in fetches[3:]:
        fetch.wait()
    w_s[2] = w_ref[2].astype(bf16)
    tails_ref[0] = k_ref[tokens - WIN :, :]
    tails_ref[1] = v_ref[tokens - WIN :, :]
    own = pl.ds(pl.multiple_of(seq_ref[0] * ROWS, ROWS), ROWS)
    for m in range(3):
        own_ref[m * ROWS : (m + 1) * ROWS, :] = w_ref[m, own, :]
    f_s[...] = columns(r_ref[...] * (-scale))

    def body(at):
        factor = f_s[at, :][:, :1]
        p3 = p3_ref[at, :]
        back = factor * mm(v_ref[at, :], w_s[2], 1, 0)
        gate, gate1, _ = gates(p1_ref[at, :])
        b_ref[at, :] = back
        d1[at, :] = (scale * back * p3 * gate1).astype(bf16)
        d3[at, :] = (scale * back * gate).astype(bf16)
        d2[at, :] = (factor * gate * p3).astype(bf16)

    blocks_of(tokens, body)
    put_grad(parts_ref, 0, k_ref, d1)
    put_grad(parts_ref, 1, k_ref, d3)
    put_grad(parts_ref, 2, v_ref, d2)


def forward_kernel(got_ref, q_ref, cot_ref, gain_ref, o_ref, p1_ref, p3_ref, sums_ref, w2_ref, w_s, s_s):
    tokens, dim = q_ref.shape
    scale = dim ** (-0.5)
    take_matrices(got_ref, w_s)
    w2_ref[...] = w_s[2]

    def body(at):
        p1 = scale * mm(q_ref[at, :], w_s[0], 1, 0)
        p3 = scale * mm(q_ref[at, :], w_s[1], 1, 0)
        gate, _, _ = gates(p1)
        out = scale * mm(gate * p3, w_s[2], 1, 1)
        p1_ref[at, :] = p1
        p3_ref[at, :] = p3
        o_ref[at, :] = out
        weighted = cot_ref[at, :].astype(f32) * gain_ref[...]
        squares = jnp.sum(out * out, axis=1, keepdims=True)
        inner = jnp.sum(weighted * out, axis=1, keepdims=True)
        lane = lax.broadcasted_iota(jnp.int32, (BLOCK, 128), 1)
        s_s[at, :] = jnp.where(lane == 0, squares, inner)

    blocks_of(tokens, body)
    sums_ref[...] = jnp.broadcast_to(s_s[...].T[:2, :], sums_ref.shape)


def backward_kernel(
    sums_ref, o_ref, p1_ref, p3_ref, q_ref, cot_ref, gain_ref, w2_ref,
    parts_ref, normed_ref, s_s, d1, d3, a_s, e_s,
):
    tokens, dim = q_ref.shape
    scale = dim ** (-0.5)
    sums = jnp.sum(sums_ref[...], axis=0)
    inverse = 1.0 / jnp.sqrt(sums[:1] / WIDTH + 1e-06)
    coef = sums[1:] * inverse * inverse * inverse / WIDTH
    s_s[0] = columns(inverse)
    s_s[1] = columns(coef)

    def body(at):
        inv = s_s[0, at, :][:, :1]
        out = o_ref[at, :]
        weighted = cot_ref[at, :].astype(f32) * gain_ref[...]
        err = (scale * (weighted * inv - out * s_s[1, at, :][:, :1])).astype(bf16)
        e_s[at, :] = err
        normed_ref[at, :] = out * inv * gain_ref[...]
        back = mm(err, w2_ref[...], 1, 0)
        p3 = p3_ref[at, :]
        gate, gate1, _ = gates(p1_ref[at, :])
        d1[at, :] = (scale * back * p3 * gate1).astype(bf16)
        d3[at, :] = (scale * back * gate).astype(bf16)
        a_s[at, :] = (gate * p3).astype(bf16)

    blocks_of(tokens, body)
    put_grad(parts_ref, 0, q_ref, d1)
    put_grad(parts_ref, 1, q_ref, d3)
    put_grad(parts_ref, 2, e_s, a_s)


def second_kernel(
    seq_ref, got_ref, k_ref, v_ref, f_s, p1_ref, p3_ref, b_ref, q_ref, normed_ref, tails_ref,
    parts_ref, layer_ref, w_s, d1, d3, d2, all_s,
):
    tokens, dim = k_ref.shape
    scale = dim ** (-0.5)
    all_s[:, :WIN, :] = tails_ref[...]
    all_s[0, WIN:, :] = k_ref[...]
    all_s[1, WIN:, :] = v_ref[...]
    span = BLOCK + WIN
    ahead = lax.broadcasted_iota(jnp.int32, (BLOCK, span), 1)
    behind = ahead - lax.broadcasted_iota(jnp.int32, (BLOCK, span), 0)
    near_by = (behind > 0) & (behind <= WIN)
    take_matrices(got_ref, w_s)

    def body(at):
        factor = f_s[at, :][:, :1]
        first_dot = scale * mm(k_ref[at, :], w_s[0], 1, 0)
        third_dot = scale * mm(k_ref[at, :], w_s[1], 1, 0)
        back_dot = factor * mm(v_ref[at, :], w_s[2], 1, 0)
        p3 = p3_ref[at, :]
        back = b_ref[at, :]
        gate, gate1, gate2 = gates(p1_ref[at, :])
        bent = gate1 * first_dot
        d1[at, :] = (
            scale
            * (gate1 * (back_dot * p3 + back * third_dot) + back * p3 * gate2 * first_dot)
        ).astype(bf16)
        d3[at, :] = (scale * (back_dot * gate + back * bent)).astype(bf16)
        d2[at, :] = (factor * (bent * p3 + gate * third_dot)).astype(bf16)
        window = pl.ds(at.start, span)
        scores = scale * mm(q_ref[at, :], all_s[0, window, :], 1, 1)
        known = near_by & (ahead + (seq_ref[0] * tokens + at.start) >= WIN)
        scores = jnp.where(known, scores, -1e30)
        expo = jnp.exp(scores - jnp.max(scores, axis=1, keepdims=True))
        probs = expo / jnp.sum(expo, axis=1, keepdims=True)
        attention = mm(probs, all_s[1, window, :], 1, 0)
        layer_ref[at, :] = (attention + normed_ref[at, :]).astype(bf16)

    blocks_of(tokens, body)
    put_grad(parts_ref, 0, k_ref, d1)
    put_grad(parts_ref, 1, k_ref, d3)
    put_grad(parts_ref, 2, v_ref, d2)


def near(array):
    return pltpu.with_memory_space_constraint(array, pltpu.VMEM)


def total_kernel(got_ref, out_ref):
    peers, height, _ = out_ref.shape
    for m in range(peers):
        out_ref[m] = totals(got_ref[:, m * height : (m + 1) * height, :]).astype(bf16)


def means(array):
    return jnp.mean(array, axis=1, keepdims=True)


def moved_kernel(got_ref, own_ref, moved_ref, out_ref):
    own = own_ref[...]
    moved = own - totals(got_ref[...])
    moved_ref[...] = moved
    factor = jnp.sqrt(means(own * own)) / jnp.sqrt(means(moved * moved) + 1e-06)
    out_ref[...] = copies((moved * factor).astype(bf16), NH)


def pulled_kernel(got_ref, own_ref, moved_ref, part_ref, out_ref):
    own, moved = own_ref[...], moved_ref[...]
    cot = totals(got_ref[...])
    target = jnp.sqrt(means(own * own))
    inverse = 1.0 / jnp.sqrt(means(moved * moved) + 1e-06)
    along = means(cot * moved) * inverse
    d_moved = (target * inverse) * (cot - moved * (along * inverse))
    part_ref[...] = d_moved + own * (along / target)
    out_ref[...] = copies(d_moved.astype(bf16), NH)


def place(arg, inputs_stay):
    if arg.dtype == jnp.int32:
        return pl.BlockSpec(memory_space=pltpu.SMEM)
    return pl.BlockSpec(memory_space=pltpu.HBM if inputs_stay else pltpu.VMEM)


def called(kernel, outs, scratch, *args, inputs_stay=False):
    return pl.pallas_call(
        kernel,
        out_shape=outs,
        in_specs=[place(arg, inputs_stay) for arg in args],
        out_specs=[pl.BlockSpec(memory_space=pltpu.VMEM)] * len(outs),
        scratch_shapes=[pltpu.VMEM(*item) if isinstance(item, tuple) else item for item in scratch],
        compiler_params=pltpu.CompilerParams(vmem_limit_bytes=VMEM_BYTES),
    )(*args)


def reduce_rows(parts):
    some = swapped(parts, PLANE)
    shape = (NH, parts.shape[1] // NH, parts.shape[2])
    (some,) = called(total_kernel, [pltpu.VMEM(shape, bf16)], [], near(some))
    return swapped(some, "zh")


def gather_rows(rows):
    some = swapped(rows, "zh")
    some = copies(some.reshape(-1, rows.shape[2]), NP)
    return swapped(some, PLANE)


def adam_step(weights, gradient, first_moment, second_moment):
    first_next = beta_one * first_moment + (1.0 - beta_one) * gradient
    second_next = beta_two * second_moment + (1.0 - beta_two) * gradient * gradient
    first_hat = first_next / (1.0 - beta_one**10)
    second_hat = second_next / (1.0 - beta_two**10)
    return (
        weights - adam_rate * first_hat / (jnp.sqrt(second_hat) + 1e-08),
        first_next,
        second_next,
    )


def inner_local(queries, keys, values, rates, gain, cotangent, fast_init, first_moment, second_moment):
    tokens, dim = queries.shape
    seq = lax.axis_index(SEQ).astype(jnp.int32).reshape(1)
    half = ((tokens, dim), bf16)
    full = pltpu.VMEM((tokens, dim), f32)
    far = jax.ShapeDtypeStruct((tokens, dim), f32)
    side = ((tokens, 128), f32)
    mats = ((3, dim, dim), bf16)
    owned = pltpu.VMEM((NP, NH * 3 * ROWS, dim), bf16)
    rows = pltpu.VMEM((3 * ROWS, dim), f32)
    alike = pltpu.VMEM((NH, 3 * ROWS, dim), bf16)
    gain_row = gain[None, :]

    parts, first_pre, third_pre, back, own, tails, factors = called(
        inner_kernel, [owned, far, far, far, rows, pltpu.VMEM((2, WIN, dim), bf16), pltpu.VMEM(*side)],
        [mats, half, half, half, half, half, ((1, tokens), f32), (mats[0], f32),
         pltpu.SemaphoreType.DMA((6,))],
        seq, *(pltpu.with_memory_space_constraint(a, pltpu.HBM) for a in (keys, values, rates, fast_init[0])),
        inputs_stay=True,
    )
    last = NY * NP - 1
    tails = lax.ppermute(tails, SEQ, [(i, i + 1) for i in range(last)])
    got = reduce_rows(parts)
    moved, out = called(moved_kernel, [rows, alike], [], near(got), near(own))
    renormed = gather_rows(out)

    fast_out, first_q, third_q, sums, second_w = called(
        forward_kernel,
        [full, full, full, pltpu.VMEM((NP, 2, tokens), f32), pltpu.VMEM(*half)], [mats, side],
        near(renormed), queries, cotangent, gain_row,
    )
    sums = swapped(sums, HEAD)
    parts, normed = called(
        backward_kernel, [owned, full], [((2, tokens, 128), f32), half, half, half, half],
        near(sums), near(fast_out), near(first_q), near(third_q), queries, cotangent, gain_row,
        near(second_w),
    )
    got = reduce_rows(parts)
    part, out = called(pulled_kernel, [rows, alike], [], near(got), near(own), near(moved))
    direction = gather_rows(out)

    parts, layer_out = called(
        second_kernel, [owned, jax.ShapeDtypeStruct(*half)],
        [mats, half, half, half, ((2, tokens + WIN, dim), bf16)],
        seq, near(direction), keys, values, near(factors), first_pre, third_pre, back, queries,
        near(normed), near(tails),
    )
    grad_rows = part - totals(reduce_rows(parts))
    shape = first_moment[0].shape
    new = adam_step(own.reshape(shape), grad_rows.reshape(shape), first_moment[0], second_moment[0])
    return (layer_out, new[0][None], new[1][None], new[2][None])


def solution(mesh):
    split = Mesh(mesh.devices.reshape(NH, 2, NY, 4, 2), ("zh", "zl", "y", "x", "c"))
    placed = (
        P(SEQ, HEAD),
        P(SEQ, HEAD),
        P(SEQ, HEAD),
        P(HEAD, SEQ),
        P(HEAD),
        P(SEQ, HEAD),
        P(HEAD, None, None, None),
        P(HEAD, None, SEQ, None),
        P(HEAD, None, SEQ, None),
    )
    return jax.shard_map(
        inner_local,
        mesh=split,
        in_specs=placed,
        out_specs=(
            P(SEQ, HEAD),
            P(HEAD, None, SEQ, None),
            P(HEAD, None, SEQ, None),
            P(HEAD, None, SEQ, None),
        ),
        check_vma=False,
    )
```

```python
import jax
import jax.numpy as jnp
from jax import lax
from jax.experimental import pallas as pl
from jax.experimental.pallas import tpu as pltpu
from jax.sharding import Mesh
from jax.sharding import PartitionSpec as P


WIN = 256
WIDTH = 4096
SEQ = ("zh", "zl", "y")
PLANE = ("zl", "y")
HEAD = ("x", "c")
NY = 4
NH = 4
NP = 8
ROWS = 16
BLOCK = 128
VMEM_BYTES = 24 * 1024 * 1024
beta_one = 0.9
beta_two = 0.95
adam_rate = 0.02
bf16 = jnp.bfloat16
f32 = jnp.float32


def mm(a, b, ca, cb):
    return lax.dot_general(
        a.astype(bf16), b.astype(bf16), (((ca,), (cb,)), ((), ())), preferred_element_type=f32
    )


def swapped(parts, axes):
    return lax.all_to_all(parts, axes, split_axis=0, concat_axis=0, tiled=True)


def copies(array, count):
    return jnp.broadcast_to(array, (count, *array.shape))


def totals(parts):
    return jnp.sum(parts.astype(f32), axis=0)


def gates(pre):
    sig = 1.0 / (1.0 + jnp.exp(-pre))
    d_sig = sig * (1.0 - sig)
    return pre * sig, sig + pre * d_sig, d_sig * (2.0 + pre * (1.0 - 2.0 * sig))


def columns(row):
    return jnp.broadcast_to(row, (128, row.shape[1])).T


def blocks_of(count, body):
    def step(j, carry):
        body(pl.ds(pl.multiple_of(j * BLOCK, BLOCK), BLOCK))
        return carry

    lax.fori_loop(0, count // BLOCK, step, 0)


def put_grad(parts_ref, number, left, right):
    grad = mm(left[...], right[...], 0, 0).astype(bf16)
    for m in range(grad.shape[0] // ROWS):
        at = (m // NP * 3 + number) * ROWS
        parts_ref[m % NP, at : at + ROWS, :] = grad[m * ROWS : (m + 1) * ROWS]


def take_matrices(parts_ref, out_ref):
    for number in range(out_ref.shape[0]):
        for m in range(out_ref.shape[1] // ROWS):
            at = (m // NP * 3 + number) * ROWS
            out_ref[number, m * ROWS : (m + 1) * ROWS, :] = parts_ref[m % NP, at : at + ROWS, :]


def inner_kernel(
    seq_ref, k_hbm, v_hbm, r_hbm, w_hbm,
    parts_ref, p1_ref, p3_ref, b_ref, own_ref, tails_ref, f_s,
    w_s, d1, d3, d2, k_ref, v_ref, r_ref, w_ref, sems,
):
    inputs = [(r_hbm, r_ref), (k_hbm, k_ref), (v_hbm, v_ref)]
    inputs += [(w_hbm.at[m], w_ref.at[m]) for m in range(3)]
    fetches = [
        pltpu.make_async_copy(source, target, sems.at[number])
        for number, (source, target) in enumerate(inputs)
    ]
    for fetch in fetches:
        fetch.start()
    for fetch in fetches:
        fetch.wait()
    tokens, dim = k_ref.shape
    tails_ref[0] = k_ref[tokens - WIN :, :]
    tails_ref[1] = v_ref[tokens - WIN :, :]
    scale = dim ** (-0.5)
    own = pl.ds(pl.multiple_of(seq_ref[0] * ROWS, ROWS), ROWS)
    for m in range(3):
        w_s[m] = w_ref[m].astype(bf16)
        own_ref[m * ROWS : (m + 1) * ROWS, :] = w_ref[m, own, :]
    f_s[...] = columns(r_ref[...] * (-scale))

    def body(at):
        factor = f_s[at, :][:, :1]
        p1 = scale * mm(k_ref[at, :], w_s[0], 1, 0)
        p3 = scale * mm(k_ref[at, :], w_s[1], 1, 0)
        back = factor * mm(v_ref[at, :], w_s[2], 1, 0)
        gate, gate1, _ = gates(p1)
        p1_ref[at, :] = p1
        p3_ref[at, :] = p3
        b_ref[at, :] = back
        d1[at, :] = (scale * back * p3 * gate1).astype(bf16)
        d3[at, :] = (scale * back * gate).astype(bf16)
        d2[at, :] = (factor * gate * p3).astype(bf16)

    blocks_of(tokens, body)
    put_grad(parts_ref, 0, k_ref, d1)
    put_grad(parts_ref, 1, k_ref, d3)
    put_grad(parts_ref, 2, v_ref, d2)


def forward_kernel(got_ref, q_ref, cot_ref, gain_ref, o_ref, p1_ref, p3_ref, sums_ref, w2_ref, w_s, s_s):
    tokens, dim = q_ref.shape
    scale = dim ** (-0.5)
    take_matrices(got_ref, w_s)
    w2_ref[...] = w_s[2]

    def body(at):
        p1 = scale * mm(q_ref[at, :], w_s[0], 1, 0)
        p3 = scale * mm(q_ref[at, :], w_s[1], 1, 0)
        gate, _, _ = gates(p1)
        out = scale * mm(gate * p3, w_s[2], 1, 1)
        p1_ref[at, :] = p1
        p3_ref[at, :] = p3
        o_ref[at, :] = out
        weighted = cot_ref[at, :].astype(f32) * gain_ref[...]
        squares = jnp.sum(out * out, axis=1, keepdims=True)
        inner = jnp.sum(weighted * out, axis=1, keepdims=True)
        lane = lax.broadcasted_iota(jnp.int32, (BLOCK, 128), 1)
        s_s[at, :] = jnp.where(lane == 0, squares, inner)

    blocks_of(tokens, body)
    sums_ref[...] = jnp.broadcast_to(s_s[...].T[:2, :], sums_ref.shape)


def backward_kernel(
    seq_ref, sums_ref, o_ref, p1_ref, p3_ref, q_ref, cot_ref, gain_ref, w2_ref, k_ref, v_ref, tails_ref,
    parts_ref, layer_ref, s_s, d1, d3, a_s, e_s, all_s,
):
    tokens, dim = q_ref.shape
    scale = dim ** (-0.5)
    all_s[:, :WIN, :] = tails_ref[...]
    all_s[0, WIN:, :] = k_ref[...]
    all_s[1, WIN:, :] = v_ref[...]
    span = BLOCK + WIN
    ahead = lax.broadcasted_iota(jnp.int32, (BLOCK, span), 1)
    behind = ahead - lax.broadcasted_iota(jnp.int32, (BLOCK, span), 0)
    near_by = (behind > 0) & (behind <= WIN)
    sums = jnp.sum(sums_ref[...], axis=0)
    inverse = 1.0 / jnp.sqrt(sums[:1] / WIDTH + 1e-06)
    coef = sums[1:] * inverse * inverse * inverse / WIDTH
    s_s[0] = columns(inverse)
    s_s[1] = columns(coef)

    def body(at):
        inv = s_s[0, at, :][:, :1]
        out = o_ref[at, :]
        weighted = cot_ref[at, :].astype(f32) * gain_ref[...]
        err = (scale * (weighted * inv - out * s_s[1, at, :][:, :1])).astype(bf16)
        e_s[at, :] = err
        window = pl.ds(at.start, span)
        scores = scale * mm(q_ref[at, :], all_s[0, window, :], 1, 1)
        known = near_by & (ahead + (seq_ref[0] * tokens + at.start) >= WIN)
        scores = jnp.where(known, scores, -1e30)
        expo = jnp.exp(scores - jnp.max(scores, axis=1, keepdims=True))
        probs = expo / jnp.sum(expo, axis=1, keepdims=True)
        attention = mm(probs, all_s[1, window, :], 1, 0)
        layer_ref[at, :] = (attention + out * inv * gain_ref[...]).astype(bf16)
        back = mm(err, w2_ref[...], 1, 0)
        p3 = p3_ref[at, :]
        gate, gate1, _ = gates(p1_ref[at, :])
        d1[at, :] = (scale * back * p3 * gate1).astype(bf16)
        d3[at, :] = (scale * back * gate).astype(bf16)
        a_s[at, :] = (gate * p3).astype(bf16)

    blocks_of(tokens, body)
    put_grad(parts_ref, 0, q_ref, d1)
    put_grad(parts_ref, 1, q_ref, d3)
    put_grad(parts_ref, 2, e_s, a_s)


def second_kernel(got_ref, k_ref, v_ref, f_s, p1_ref, p3_ref, b_ref, parts_ref, w_s, d1, d3, d2):
    tokens, dim = k_ref.shape
    scale = dim ** (-0.5)
    take_matrices(got_ref, w_s)

    def body(at):
        factor = f_s[at, :][:, :1]
        first_dot = scale * mm(k_ref[at, :], w_s[0], 1, 0)
        third_dot = scale * mm(k_ref[at, :], w_s[1], 1, 0)
        back_dot = factor * mm(v_ref[at, :], w_s[2], 1, 0)
        p3 = p3_ref[at, :]
        back = b_ref[at, :]
        gate, gate1, gate2 = gates(p1_ref[at, :])
        bent = gate1 * first_dot
        d1[at, :] = (
            scale
            * (gate1 * (back_dot * p3 + back * third_dot) + back * p3 * gate2 * first_dot)
        ).astype(bf16)
        d3[at, :] = (scale * (back_dot * gate + back * bent)).astype(bf16)
        d2[at, :] = (factor * (bent * p3 + gate * third_dot)).astype(bf16)

    blocks_of(tokens, body)
    put_grad(parts_ref, 0, k_ref, d1)
    put_grad(parts_ref, 1, k_ref, d3)
    put_grad(parts_ref, 2, v_ref, d2)


def near(array):
    return pltpu.with_memory_space_constraint(array, pltpu.VMEM)


def total_kernel(got_ref, out_ref):
    peers, height, _ = out_ref.shape
    for m in range(peers):
        out_ref[m] = totals(got_ref[:, m * height : (m + 1) * height, :]).astype(bf16)


def means(array):
    return jnp.mean(array, axis=1, keepdims=True)


def moved_kernel(got_ref, own_ref, moved_ref, out_ref):
    own = own_ref[...]
    moved = own - totals(got_ref[...])
    moved_ref[...] = moved
    factor = jnp.sqrt(means(own * own)) / jnp.sqrt(means(moved * moved) + 1e-06)
    out_ref[...] = copies((moved * factor).astype(bf16), NH)


def pulled_kernel(got_ref, own_ref, moved_ref, part_ref, out_ref):
    own, moved = own_ref[...], moved_ref[...]
    cot = totals(got_ref[...])
    target = jnp.sqrt(means(own * own))
    inverse = 1.0 / jnp.sqrt(means(moved * moved) + 1e-06)
    along = means(cot * moved) * inverse
    d_moved = (target * inverse) * (cot - moved * (along * inverse))
    part_ref[...] = d_moved + own * (along / target)
    out_ref[...] = copies(d_moved.astype(bf16), NH)


def place(arg, inputs_stay):
    if arg.dtype == jnp.int32:
        return pl.BlockSpec(memory_space=pltpu.SMEM)
    return pl.BlockSpec(memory_space=pltpu.HBM if inputs_stay else pltpu.VMEM)


def called(kernel, outs, scratch, *args, inputs_stay=False):
    return pl.pallas_call(
        kernel,
        out_shape=outs,
        in_specs=[place(arg, inputs_stay) for arg in args],
        out_specs=[pl.BlockSpec(memory_space=pltpu.VMEM)] * len(outs),
        scratch_shapes=[pltpu.VMEM(*item) if isinstance(item, tuple) else item for item in scratch],
        compiler_params=pltpu.CompilerParams(vmem_limit_bytes=VMEM_BYTES),
    )(*args)


def reduce_rows(parts):
    some = swapped(parts, PLANE)
    shape = (NH, parts.shape[1] // NH, parts.shape[2])
    (some,) = called(total_kernel, [pltpu.VMEM(shape, bf16)], [], near(some))
    return swapped(some, "zh")


def gather_rows(rows):
    some = swapped(rows, "zh")
    some = copies(some.reshape(-1, rows.shape[2]), NP)
    return swapped(some, PLANE)


def adam_step(weights, gradient, first_moment, second_moment):
    first_next = beta_one * first_moment + (1.0 - beta_one) * gradient
    second_next = beta_two * second_moment + (1.0 - beta_two) * gradient * gradient
    first_hat = first_next / (1.0 - beta_one**10)
    second_hat = second_next / (1.0 - beta_two**10)
    return (
        weights - adam_rate * first_hat / (jnp.sqrt(second_hat) + 1e-08),
        first_next,
        second_next,
    )


def inner_local(queries, keys, values, rates, gain, cotangent, fast_init, first_moment, second_moment):
    tokens, dim = queries.shape
    seq = lax.axis_index(SEQ).astype(jnp.int32).reshape(1)
    half = ((tokens, dim), bf16)
    full = pltpu.VMEM((tokens, dim), f32)
    far = jax.ShapeDtypeStruct((tokens, dim), f32)
    side = ((tokens, 128), f32)
    mats = ((3, dim, dim), bf16)
    owned = pltpu.VMEM((NP, NH * 3 * ROWS, dim), bf16)
    rows = pltpu.VMEM((3 * ROWS, dim), f32)
    alike = pltpu.VMEM((NH, 3 * ROWS, dim), bf16)
    gain_row = gain[None, :]

    parts, first_pre, third_pre, back, own, tails, factors = called(
        inner_kernel, [owned, far, far, far, rows, pltpu.VMEM((2, WIN, dim), bf16), pltpu.VMEM(*side)],
        [mats, half, half, half, half, half, ((1, tokens), f32), (mats[0], f32),
         pltpu.SemaphoreType.DMA((6,))],
        seq, *(pltpu.with_memory_space_constraint(a, pltpu.HBM) for a in (keys, values, rates, fast_init[0])),
        inputs_stay=True,
    )
    last = NY * NP - 1
    tails = lax.ppermute(tails, SEQ, [(i, i + 1) for i in range(last)])
    got = reduce_rows(parts)
    moved, out = called(moved_kernel, [rows, alike], [], near(got), near(own))
    renormed = gather_rows(out)

    fast_out, first_q, third_q, sums, second_w = called(
        forward_kernel,
        [full, full, full, pltpu.VMEM((NP, 2, tokens), f32), pltpu.VMEM(*half)], [mats, side],
        near(renormed), queries, cotangent, gain_row,
    )
    sums = swapped(sums, HEAD)
    parts, layer_out = called(
        backward_kernel, [owned, jax.ShapeDtypeStruct(*half)],
        [((2, tokens, 128), f32), half, half, half, half, ((2, tokens + WIN, dim), bf16)],
        seq, near(sums), near(fast_out), near(first_q), near(third_q), queries, cotangent, gain_row,
        near(second_w), keys, values, tails,
    )
    got = reduce_rows(parts)
    part, out = called(pulled_kernel, [rows, alike], [], near(got), near(own), near(moved))
    direction = gather_rows(out)

    (parts,) = called(
        second_kernel, [owned], [mats, half, half, half],
        near(direction), keys, values, near(factors), first_pre, third_pre, back,
    )
    grad_rows = part - totals(reduce_rows(parts))
    shape = first_moment[0].shape
    new = adam_step(own.reshape(shape), grad_rows.reshape(shape), first_moment[0], second_moment[0])
    return (layer_out, new[0][None], new[1][None], new[2][None])


def solution(mesh):
    split = Mesh(mesh.devices.reshape(NH, 2, NY, 4, 2), ("zh", "zl", "y", "x", "c"))
    placed = (
        P(SEQ, HEAD),
        P(SEQ, HEAD),
        P(SEQ, HEAD),
        P(HEAD, SEQ),
        P(HEAD),
        P(SEQ, HEAD),
        P(HEAD, None, None, None),
        P(HEAD, None, SEQ, None),
        P(HEAD, None, SEQ, None),
    )
    return jax.shard_map(
        inner_local,
        mesh=split,
        in_specs=placed,
        out_specs=(
            P(SEQ, HEAD),
            P(HEAD, None, SEQ, None),
            P(HEAD, None, SEQ, None),
            P(HEAD, None, SEQ, None),
        ),
        check_vma=False,
    )
```
